128 devices in a mesh: rows: 16 (over z_lo, x, core), batch: 8 (over z_hi, y).
Axes of the slice: x: 4, y: 4, z: 4 (z_hi: 2, z_lo: 2; z = z_hi * 2 + z_lo), core: 2. Of those that a mesh axis runs over, the one named last changes fastest.
Arguments:
- bases: bfloat16 [49152, 2048], P('rows', 'batch'), may hold values from -30 to 30
- start: float32 [2048, 512], P('batch'), may hold values from -6 to 6
Outputs:
- modes: bfloat16 [49152, 512], P(('rows', 'batch'))
The draws below stay inside these ranges and needn't reach their ends.
All inputs are finite; a program needn't handle non-finite values.
Results may differ from the reference program's by a relative error of at most 0.0041.
Values may be sent and summed in bfloat16 or wider, within the bound.
A program may use at most 128 MiB of HBM per device.

```python
import math
import jax
import jax.numpy as jnp
from jax import lax

R = 256
M = 512
ITERS = 2
ROWS_DEV = 3072
COLS = 2048
ROWS = 49152


def draw_bases(key, part):
    base_key = jax.random.fold_in(key, 17)
    keys = jax.random.split(base_key, 4)
    row_pos = jnp.arange(ROWS, dtype=jnp.float32) / ROWS
    shared = jax.random.truncated_normal(keys[0], -4.0, 4.0, (ROWS, R), jnp.float32)
    own_part = jax.random.truncated_normal(keys[1], -4.0, 4.0, (ROWS, COLS), jnp.float32)
    row_scale = jnp.exp(jax.random.uniform(keys[2], (ROWS,), jnp.float32, math.log(0.3), math.log(3.0)) + 0.55 * row_pos)
    shared_weight = 0.5
    own_weight = 0.65
    col_scale = jnp.exp(jax.random.uniform(keys[3], (COLS,), jnp.float32, math.log(0.6), math.log(1.8)))
    mixed = shared_weight * jnp.tile(shared, (1, COLS // R)) + own_weight * own_part
    return (0.5 * mixed * row_scale[:, None] * col_scale[None, :]).astype(jnp.bfloat16)


def shard_levels(key, dims, shards, least, high):
    def one(dim, blocks):
        steps = jax.random.uniform(jax.random.fold_in(jax.random.fold_in(key, 6), dim), (blocks,), jnp.float32, least / len(shards), high / len(shards))
        return jnp.repeat(jnp.exp(steps), dims[dim] // blocks).reshape((-1,) + (1,) * (len(dims) - dim - 1))

    gain = one(*shards[0])
    for cut in shards[1:]:
        gain = gain * one(*cut)
    return gain


def centred(rng, shape, spread, most, cuts=(), kind=jnp.bfloat16):
    level = shard_levels(rng, shape, cuts, -0.22, 0.18) if cuts else 1.0
    values = jax.random.normal(rng, shape, jnp.float32) * spread * level
    return jnp.minimum(jnp.maximum(values, -most), most).astype(kind)


def setup_inputs(seed: int = 0) -> dict:
    arg_keys = jax.random.split(jax.random.key(seed), 3)
    return {
        "bases": draw_bases(jax.random.fold_in(arg_keys[2], 71), 0),
        "start": centred(arg_keys[1], (COLS, M), 1.0, 6.0, ((0, 8),), jnp.float32),
    }


def reference(bases, start):
    row_blocks = bases.reshape(ROWS // ROWS_DEV, ROWS_DEV, COLS)

    def accumulate(carry, row_block):
        gram_matrix, energy = carry
        gram_matrix = gram_matrix + lax.dot_general(row_block.astype(jnp.float32), row_block.astype(jnp.float32), (((0,), (0,)), ((), ())), preferred_element_type=jnp.float32)
        energy = energy + jnp.sum(jnp.square(row_block.astype(jnp.float32)))
        return ((gram_matrix, energy), None)
    initial = (jnp.zeros((COLS, COLS), jnp.float32), jnp.zeros((), jnp.float32))
    (gram_matrix, energy), unused_out = lax.scan(accumulate, initial, row_blocks)
    diag_mean = energy / COLS
    q_now = start
    for iteration in range(ITERS):
        lifted = jnp.dot(gram_matrix, q_now, precision=lax.Precision.HIGHEST) / diag_mean + q_now
        correlation = lax.dot_general(lifted, lifted, (((0,), (0,)), ((), ())), precision=lax.Precision.HIGHEST)
        factor = jnp.linalg.cholesky(correlation)
        q_now = jax.scipy.linalg.solve_triangular(factor, lifted.T, lower=True).T
    q_low = q_now.astype(jnp.bfloat16)
    modes = jnp.dot(bases.astype(jnp.float32), q_low.astype(jnp.float32), preferred_element_type=jnp.float32)
    return modes.astype(jnp.bfloat16)
```

```python
import functools

import jax
import jax.numpy as jnp
from jax import lax
from jax.experimental import pallas as pl
from jax.experimental.pallas import tpu as pltpu
from jax.sharding import PartitionSpec as P

ITERS = 2
NB = 128
HIGHEST = lax.Precision.HIGHEST
VMEM_SPEC = pl.BlockSpec(memory_space=pltpu.VMEM)


def dot_f32(left, right, left_dim, right_dim):
    return lax.dot_general(
        left, right, (((left_dim,), (right_dim,)), ((), ())),
        precision=HIGHEST, preferred_element_type=jnp.float32,
    )


def dot_low(left, right, left_dim, right_dim):
    return lax.dot_general(
        left, right, (((left_dim,), (right_dim,)), ((), ())),
        preferred_element_type=jnp.float32,
    )


def split(value):
    high = value.astype(jnp.bfloat16)
    return high, (value - high.astype(jnp.float32)).astype(jnp.bfloat16)


def factor_block(aug, work):
    row = lax.broadcasted_iota(jnp.int32, (8, NB), 0)
    for panel in range(NB // 8):
        low = 8 * panel
        left = aug[low:low + 8, :NB]
        right = aug[low:low + 8, NB:]
        cols = [jnp.broadcast_to(left[:, low + j:low + j + 1], (8, NB)) for j in range(8)]
        pivots = jnp.zeros((8, NB), jnp.float32)
        for k in range(8):
            pivot = jnp.broadcast_to(cols[k][k:k + 1, :], (8, NB))
            mult = jnp.where(row > k, cols[k] / pivot, 0.0)
            pivots = jnp.where(row == k, pivot, pivots)
            for j in range(k + 1, 8):
                cols[j] = cols[j] - mult * jnp.broadcast_to(cols[j][k:k + 1, :], (8, NB))
            left = left - mult * jnp.broadcast_to(left[k:k + 1, :], (8, NB))
            right = right - mult * jnp.broadcast_to(right[k:k + 1, :], (8, NB))
        scale = lax.rsqrt(pivots)
        rows = jnp.concatenate([left * scale, right * scale], axis=1)
        work[low:low + 8, :] = rows
        if low + 8 < NB:
            aug[low + 8:, :] = aug[low + 8:, :] - dot_f32(rows[:, :NB], rows, 0, 0)[low + 8:, :]


def factor_kernel(n, c_ref, t_ref, rest, upper, aug, work, inverses):
    blocks = n // NB
    rest[...] = c_ref[...]
    t_ref[...] = jnp.zeros_like(t_ref)
    row = lax.broadcasted_iota(jnp.int32, (NB, NB), 0)
    col = lax.broadcasted_iota(jnp.int32, (NB, NB), 1)

    @pl.loop(0, blocks)
    def _(j):
        here = pl.ds(pl.multiple_of(j * NB, NB), NB)
        aug[:, :NB] = rest[here, here]
        aug[:, NB:] = jnp.where(row == col, 1.0, 0.0)
        factor_block(aug, work)
        inverse = jnp.where(row >= col, work[:, NB:], 0.0)
        inverses[j] = inverse
        rows = dot_f32(inverse, rest[here, :], 1, 0)
        upper[here, :] = rows

        @pl.when(j < blocks - 1)
        def _():
            rest[...] = rest[...] - dot_f32(rows, rows, 0, 0)

    for j in range(blocks):
        here = slice(j * NB, (j + 1) * NB)
        block = inverses[j].T
        t_ref[here, here] = block
        if j:
            above = slice(0, j * NB)
            t_ref[above, here] = -dot_f32(
                t_ref[above, above], dot_f32(upper[above, here], block, 1, 0), 1, 0
            )


def inverse_factor(correlation):
    n = correlation.shape[0]
    return pl.pallas_call(
        functools.partial(factor_kernel, n),
        out_shape=jax.ShapeDtypeStruct((n, n), jnp.float32),
        in_specs=[VMEM_SPEC],
        out_specs=VMEM_SPEC,
        scratch_shapes=[
            pltpu.VMEM((n, n), jnp.float32),
            pltpu.VMEM((n, n), jnp.float32),
            pltpu.VMEM((NB, 2 * NB), jnp.float32),
            pltpu.VMEM((NB, 2 * NB), jnp.float32),
            pltpu.VMEM((n // NB, NB, NB), jnp.float32),
        ],
    )(correlation)


def gram_kernel(a_ref, q_ref, out_ref):
    a = a_ref[...]
    high, low = split(q_ref[...])
    inner = dot_low(a, high, 1, 0) + dot_low(a, low, 1, 0)
    high, low = split(inner)
    out_ref[...] = dot_low(a, high, 0, 0) + dot_low(a, low, 0, 0)


def gram_apply(a, q):
    return pl.pallas_call(
        gram_kernel,
        out_shape=jax.ShapeDtypeStruct(q.shape, jnp.float32),
        in_specs=[VMEM_SPEC, VMEM_SPEC],
        out_specs=VMEM_SPEC,
    )(a, q)


def on_device(bases, start):
    basis_width = bases.shape[1]
    all_columns = basis_width * lax.axis_size("batch")
    own_rows = lax.all_to_all(bases, "batch", split_axis=0, concat_axis=1, tiled=True)
    energy = lax.psum(jnp.sum(jnp.square(own_rows.astype(jnp.float32))), ("rows", "batch"))
    diag_mean = energy / all_columns
    q = lax.all_gather(start, "batch", axis=0, tiled=True)
    for iteration in range(ITERS):
        lifted = lax.psum(gram_apply(own_rows, q), ("rows", "batch")) / diag_mean + q
        correlation = dot_f32(lifted, lifted, 0, 0)
        q = dot_f32(lifted, inverse_factor(correlation), 1, 0)
    q_low = q.astype(jnp.bfloat16)
    return jnp.dot(own_rows, q_low, preferred_element_type=jnp.float32).astype(jnp.bfloat16)


def solution(mesh):
    in_specs = (P("rows", "batch"), P("batch", None))
    out_specs = P(("rows", "batch"), None)
    return jax.shard_map(
        on_device, mesh=mesh, in_specs=in_specs, out_specs=out_specs, check_vma=False
    )
```

```python
import functools

import jax
import jax.numpy as jnp
from jax import lax
from jax.experimental import pallas as pl
from jax.experimental.pallas import tpu as pltpu
from jax.sharding import PartitionSpec as P

NB = 128
RING = 4
ORDERS = (("x", "y", "z"), ("y", "z", "x"), ("z", "x", "y"))
UNITS = (24, 24, 16)
HIGHEST = lax.Precision.HIGHEST
VMEM_SPEC = pl.BlockSpec(memory_space=pltpu.VMEM)
F32, BF16 = jnp.float32, jnp.bfloat16


def dot_f32(left, right, left_dim, right_dim):
    return lax.dot_general(
        left, right, (((left_dim,), (right_dim,)), ((), ())),
        precision=HIGHEST, preferred_element_type=F32,
    )


def dot_low(left, right, left_dim, right_dim):
    return lax.dot_general(
        left, right, (((left_dim,), (right_dim,)), ((), ())), preferred_element_type=F32
    )


def split(value):
    high = value.astype(BF16)
    return high, (value - high.astype(F32)).astype(BF16)


def position():
    rows, batch = lax.axis_index("rows"), lax.axis_index("batch")
    return {
        "x": rows // 2 % 4,
        "y": batch % 4,
        "z": batch // 4 * 2 + rows // 8,
        "core": rows % 2,
    }


def device_at(pos):
    return {
        "rows": pos["z"] % 2 * 8 + pos["x"] * 2 + pos["core"],
        "batch": pos["z"] // 2 * 4 + pos["y"],
    }


def ring_peer(pos, axis, distance):
    there = dict(pos)
    there[axis] = (pos[axis] + distance) % RING
    return there


def sibling(pos):
    there = dict(pos)
    there["core"] = 1 - pos["core"]
    return there


def greet(peers):
    barrier = pltpu.get_barrier_semaphore()
    for peer in peers:
        pl.semaphore_signal(
            barrier, inc=1, device_id=device_at(peer), device_id_type=pl.DeviceIdType.MESH
        )
    pl.semaphore_wait(barrier, len(peers))


class Copies:
    def __init__(self, send_sem, recv_sem):
        self.send_sem, self.recv_sem, self.made = send_sem, recv_sem, []

    def start(self, src, dst, peer):
        index = len(self.made)
        copy = pltpu.make_async_remote_copy(
            src_ref=src, dst_ref=dst,
            send_sem=self.send_sem.at[index], recv_sem=self.recv_sem.at[index],
            device_id=device_at(peer), device_id_type=pl.DeviceIdType.MESH,
        )
        copy.start()
        self.made.append(copy)
        return copy

    def finish(self):
        for copy in self.made:
            copy.wait_send()


def exchange_kernel(
    bases_ref, start_ref, a_ref, q_ref, energy_ref, e_send, e_recv, send_sem, recv_sem, own_sem
):
    pos = position()
    core, x = pos["core"], pos["x"]
    batch = lax.axis_index("batch")
    count = lax.axis_size("batch")
    height = bases_ref.shape[0] // count
    width = bases_ref.shape[1]
    quarter = start_ref.shape[0] // RING
    partners = []
    for distance in range(1, count):
        other = (batch + distance) % count
        there = dict(pos)
        there["y"] = other % 4
        there["z"] = other // 4 * 2 + pos["z"] % 2
        partners.append(there)
    x_peers = [ring_peer(pos, "x", d) for d in (1, 2, 3)]
    y_peers = [ring_peer(pos, "y", d) for d in (1, 2, 3)]
    z_peers = [ring_peer(pos, "z", d) for d in (1, 2, 3)]
    z_others = [z_peers[0], z_peers[2]]
    greet(partners + x_peers + z_others + [sibling(pos)])
    copies = Copies(send_sem, recv_sem)

    own_rows = pl.ds(pl.multiple_of(core * height, height), height)
    my_rows = pl.ds(pl.multiple_of(x * quarter, quarter), quarter)

    def columns(which):
        return pl.ds(pl.multiple_of(which * width, width), width)

    start_copies = []
    for half in range(2):
        here = pl.ds(pl.multiple_of(core * 256 + half * 128, 128), 128)
        own = pltpu.make_async_copy(
            start_ref.at[my_rows, here], q_ref.at[batch, half, my_rows, :], own_sem.at[half]
        )
        own.start()
        start_copies.append(own)
    start_in = []
    for there in partners:
        for half in range(2):
            here = pl.ds(pl.multiple_of(core * 256 + half * 128, 128), 128)
            start_in.append(copies.start(
                start_ref.at[my_rows, here], q_ref.at[batch, half, my_rows, :], there
            ))
    block_in = []
    for distance, there in enumerate(partners, 1):
        other = (batch + distance) % count
        rows = pl.ds(pl.multiple_of(other * height, height), height)
        block_in.append(copies.start(
            bases_ref.at[rows, :], a_ref.at[own_rows, columns(batch)], there
        ))
    rows = pl.ds(pl.multiple_of(batch * height, height), height)
    own = pltpu.make_async_copy(
        bases_ref.at[rows, :], a_ref.at[own_rows, columns(batch)], own_sem.at[2]
    )
    own.start()
    aside = [copies.start(
        bases_ref.at[rows, :], a_ref.at[own_rows, columns(batch)], sibling(pos)
    )]

    def add_square(step, total):
        low = pl.multiple_of(step * 64, 64)
        value = bases_ref[pl.ds(low, 64), :].astype(F32)
        value = value * value
        return total + jnp.sum(value.reshape(8, 8, 2 * 128), axis=0)

    total = lax.fori_loop(
        0, bases_ref.shape[0] // 64, add_square, jnp.zeros((8, 2 * 128), F32)
    )
    total = total[:, :128] + total[:, 128:]

    for copy in start_copies:
        copy.wait()
    for copy in start_in:
        copy.wait_recv()
    x_in = [
        copies.start(q_ref.at[:, :, my_rows, :], q_ref.at[:, :, my_rows, :], there)
        for there in x_peers
    ]
    for stage, peers in enumerate((x_peers, y_peers, z_peers, [sibling(pos)])):
        e_send[stage] = total
        incoming = [
            copies.start(e_send.at[stage], e_recv.at[stage, slot], there)
            for slot, there in enumerate(peers)
        ]
        for slot, copy in enumerate(incoming):
            copy.wait_recv()
            total = total + e_recv[stage, slot]
    energy_ref[...] = jnp.broadcast_to(jnp.sum(total, keepdims=True), energy_ref.shape)

    for distance, copy in enumerate(block_in, 1):
        copy.wait_recv()
        other = (batch + count - distance) % count
        block = a_ref.at[own_rows, columns(other)]
        aside.append(copies.start(block, block, sibling(pos)))
    own.wait()
    for copy in x_in + aside:
        copy.wait_recv()
    copies.finish()


EXCHANGE_COPIES = 14 + 7 + 1 + 3 + 10 + 7


def exchange(bases, start, count):
    height = bases.shape[0] // count
    sems = pltpu.SemaphoreType.DMA((EXCHANGE_COPIES,))
    return pl.pallas_call(
        exchange_kernel,
        out_shape=(
            jax.ShapeDtypeStruct((2 * height, bases.shape[1] * count), BF16),
            jax.ShapeDtypeStruct((count, 2, start.shape[0], 128), F32),
            jax.ShapeDtypeStruct((8, 128), F32),
        ),
        in_specs=[VMEM_SPEC] * 2,
        out_specs=(VMEM_SPEC,) * 3,
        scratch_shapes=[
            pltpu.VMEM((4, 8, 128), F32),
            pltpu.VMEM((4, 3, 8, 128), F32),
            sems,
            sems,
            pltpu.SemaphoreType.DMA((3,)),
        ],
        compiler_params=pltpu.CompilerParams(collective_id=0, has_side_effects=True),
    )(bases, start)


def reduce_kernel(
    diag_columns, part_ref, q_ref, energy_ref, out_ref, work, *scratch
):
    slots, (send_sem, recv_sem) = scratch[:9], scratch[9:]
    pos = position()
    core = pos["core"]
    peers = {axis: [ring_peer(pos, axis, d) for d in (1, 2, 3)] for axis in "xyz"}
    greet(peers["x"] + peers["y"] + peers["z"] + [sibling(pos)])
    copies = Copies(send_sem, recv_sem)
    scale = diag_columns / energy_ref[0:1, :]
    bases = [64 * sum(UNITS[:k]) for k in range(3)]
    sizes = [[16 * u, 4 * u, u] for u in UNITS]

    def rows(start, size):
        return pl.ds(pl.multiple_of(start, 8), size)

    def send_sums(k, stage, source, origin):
        axis, size = ORDERS[k][stage], sizes[k][stage]
        return [
            copies.start(
                source.at[rows(origin + (pos[axis] + d) % RING * size, size), :],
                slots[3 * k + stage].at[d - 1],
                peers[axis][d - 1],
            )
            for d in (1, 2, 3)
        ]

    origin = list(bases)
    flight = [send_sums(k, 0, part_ref, origin[k]) for k in range(3)]
    for stage in range(3):
        for k in range(3):
            axis, size = ORDERS[k][stage], sizes[k][stage]
            for copy in flight[k]:
                copy.wait_recv()
            origin[k] = origin[k] + pos[axis] * size
            here = rows(origin[k], size)
            source = part_ref if stage == 0 else work
            slot = slots[3 * k + stage]
            value = source[here, :] + slot[0] + slot[1] + slot[2]
            if stage < 2:
                work[here, :] = value
                flight[k] = send_sums(k, stage + 1, work, origin[k])
            else:
                out_ref[core, here, :] = value * scale + q_ref[core, here, :]
                block = out_ref.at[core, here, :]
                flight[k] = [copies.start(block, block, there) for there in peers[axis]]
    aside = []
    for stage in (2, 1, 0):
        for k in range(3):
            axis, size = ORDERS[k][stage], sizes[k][stage]
            origin[k] = origin[k] - pos[axis] * size
            if stage:
                for copy in flight[k]:
                    copy.wait_recv()
                block = out_ref.at[core, rows(origin[k], 4 * size), :]
                flight[k] = [
                    copies.start(block, block, there) for there in peers[ORDERS[k][stage - 1]]
                ]
                if stage == 1:
                    aside.append(copies.start(block, block, sibling(pos)))
            else:
                for d, copy in zip((1, 2, 3), flight[k]):
                    copy.wait_recv()
                    sender = (pos[axis] + RING - d) % RING
                    block = out_ref.at[core, rows(origin[k] + sender * size, size), :]
                    aside.append(copies.start(block, block, sibling(pos)))
    for copy in aside:
        copy.wait_recv()
    copies.finish()


REDUCE_COPIES = 9 * 3 + 9 * 3 + 3 + 9


def reduce_all(part, q, energy, diag_columns, collective_id):
    sems = pltpu.SemaphoreType.DMA((REDUCE_COPIES,))
    slots = [
        pltpu.VMEM((3, size * u, 128), F32) for u in UNITS for size in (16, 4, 1)
    ]
    return pl.pallas_call(
        functools.partial(reduce_kernel, diag_columns),
        out_shape=jax.ShapeDtypeStruct((2,) + part.shape, F32),
        in_specs=[VMEM_SPEC] * 3,
        out_specs=VMEM_SPEC,
        scratch_shapes=[pltpu.VMEM(part.shape, F32), *slots, sems, sems],
        compiler_params=pltpu.CompilerParams(
            collective_id=collective_id, has_side_effects=True
        ),
    )(part, q, energy)


def apply_kernel(a_ref, q_ref, part_ref):
    core = lax.axis_index("rows") % 2
    blocks = q_ref.shape[1] // 512
    high, low = [], []
    for block in range(blocks):
        value = jnp.concatenate(
            [q_ref[core, block * 512 + half * 256:block * 512 + half * 256 + 256, :]
             for half in range(2)], axis=1)
        one, two = split(value)
        high.append(one)
        low.append(two)
    high, low = jnp.concatenate(high, axis=0), jnp.concatenate(low, axis=0)
    a = a_ref[...]
    high, low = split(dot_low(a, high, 1, 0) + dot_low(a, low, 1, 0))
    for block in range(blocks):
        columns = a_ref[:, block * 256:(block + 1) * 256]
        value = dot_low(columns, high, 0, 0) + dot_low(columns, low, 0, 0)
        for half in range(2):
            part_ref[block * 512 + half * 256:block * 512 + half * 256 + 256, :] = (
                value[:, half * 128:(half + 1) * 128])


def apply_gram(a, q):
    return pl.pallas_call(
        apply_kernel,
        out_shape=jax.ShapeDtypeStruct(q.shape[1:], F32),
        in_specs=[VMEM_SPEC] * 2,
        out_specs=VMEM_SPEC,
    )(a, q)


def factor_block(aug, work):
    row = lax.broadcasted_iota(jnp.int32, (8, NB), 0)
    for panel in range(NB // 8):
        low = 8 * panel
        left = aug[low:low + 8, :NB]
        right = aug[low:low + 8, NB:]
        cols = [jnp.broadcast_to(left[:, low + j:low + j + 1], (8, NB)) for j in range(8)]
        pivots = jnp.zeros((8, NB), F32)
        for k in range(8):
            pivot = jnp.broadcast_to(cols[k][k:k + 1, :], (8, NB))
            mult = jnp.where(row > k, cols[k] / pivot, 0.0)
            pivots = jnp.where(row == k, pivot, pivots)
            for j in range(k + 1, 8):
                cols[j] = cols[j] - mult * jnp.broadcast_to(cols[j][k:k + 1, :], (8, NB))
            left = left - mult * jnp.broadcast_to(left[k:k + 1, :], (8, NB))
            right = right - mult * jnp.broadcast_to(right[k:k + 1, :], (8, NB))
        scale = lax.rsqrt(pivots)
        rows = jnp.concatenate([left * scale, right * scale], axis=1)
        work[low:low + 8, :] = rows
        if low + 8 < NB:
            aug[low + 8:, :] = aug[low + 8:, :] - dot_f32(rows[:, :NB], rows, 0, 0)[low + 8:, :]


def inverse_factor(t_ref, rest, upper, aug, work, inverses):
    n = rest.shape[0]
    blocks = n // NB
    t_ref[...] = jnp.zeros_like(t_ref)
    row = lax.broadcasted_iota(jnp.int32, (NB, NB), 0)
    col = lax.broadcasted_iota(jnp.int32, (NB, NB), 1)

    @pl.loop(0, blocks)
    def _(j):
        here = pl.ds(pl.multiple_of(j * NB, NB), NB)
        aug[:, :NB] = rest[here, here]
        aug[:, NB:] = jnp.where(row == col, 1.0, 0.0)
        factor_block(aug, work)
        inverse = jnp.where(row >= col, work[:, NB:], 0.0)
        inverses[j] = inverse
        rows = dot_f32(inverse, rest[here, :], 1, 0)
        upper[here, :] = rows

        @pl.when(j < blocks - 1)
        def _():
            rest[...] = rest[...] - dot_f32(rows, rows, 0, 0)

    for j in range(blocks):
        here = slice(j * NB, (j + 1) * NB)
        block = inverses[j].T
        t_ref[here, here] = block
        if j:
            above = slice(0, j * NB)
            t_ref[above, here] = -dot_f32(
                t_ref[above, above], dot_f32(upper[above, here], block, 1, 0), 1, 0
            )


def tile_rows(lifted_ref, block):
    low = block * 512
    return jnp.concatenate(
        [lifted_ref[core, low + half * 256:low + half * 256 + 256, :]
         for core in range(2) for half in range(2)], axis=1)


def dot_split(left, right):
    left_high, left_low = split(left)
    right_high, right_low = split(right)
    return (dot_low(left_high, right_high, 1, 0) + dot_low(left_low, right_high, 1, 0)
            + dot_low(left_high, right_low, 1, 0))


def add_correlation(rest, high, low):
    cross = dot_low(high, low, 0, 0)
    rest[...] += dot_low(high, high, 0, 0) + cross + cross.T


def first_kernel(lifted_ref, t_ref, rest, *scratch):
    rest[...] = jnp.zeros_like(rest)
    for block in range(lifted_ref.shape[1] // 512):
        add_correlation(rest, *split(tile_rows(lifted_ref, block)))
    inverse_factor(t_ref, rest, *scratch)


def last_kernel(lifted_ref, first_ref, a_ref, modes_ref, t_ref, second, rest, *scratch):
    blocks = lifted_ref.shape[1] // 512
    rest[...] = jnp.zeros_like(rest)
    first = first_ref[...]
    for block in range(blocks):
        value = dot_split(tile_rows(lifted_ref, block), first)
        second[block * 256:(block + 1) * 256, :] = value
        add_correlation(rest, *split(value))
    inverse_factor(t_ref, rest, *scratch)
    height = modes_ref.shape[0]
    core = lax.axis_index("rows") % 2
    own_rows = pl.ds(pl.multiple_of(core * height, height), height)
    t = t_ref[...]
    total = jnp.zeros(modes_ref.shape, F32)
    for block in range(blocks):
        q_low = dot_split(second[block * 256:(block + 1) * 256, :], t).astype(BF16)
        total = total + dot_low(a_ref[own_rows, block * 256:(block + 1) * 256], q_low, 1, 0)
    modes_ref[...] = total.astype(BF16)


def factor_scratch(n):
    return [
        pltpu.VMEM((n, n), F32),
        pltpu.VMEM((n, n), F32),
        pltpu.VMEM((NB, 2 * NB), F32),
        pltpu.VMEM((NB, 2 * NB), F32),
        pltpu.VMEM((n // NB, NB, NB), F32),
    ]


def on_device(bases, start):
    count = lax.axis_size("batch")
    n = start.shape[1]
    all_columns = bases.shape[1] * count
    a, q, energy = exchange(bases, start, count)
    q = q.reshape(1, -1, 128)
    q = jnp.concatenate([q, q], axis=0)
    first = reduce_all(apply_gram(a, q), q, energy, float(all_columns), 1)
    t_first = pl.pallas_call(
        first_kernel,
        out_shape=jax.ShapeDtypeStruct((n, n), F32),
        in_specs=[VMEM_SPEC],
        out_specs=VMEM_SPEC,
        scratch_shapes=factor_scratch(n),
    )(first)
    second = reduce_all(apply_gram(a, first), first, energy, float(all_columns), 2)
    return pl.pallas_call(
        last_kernel,
        out_shape=jax.ShapeDtypeStruct((a.shape[0] // 2, n), BF16),
        in_specs=[VMEM_SPEC] * 3,
        out_specs=VMEM_SPEC,
        scratch_shapes=[
            pltpu.VMEM((n, n), F32), pltpu.VMEM((all_columns, n), F32), *factor_scratch(n)
        ],
    )(second, t_first, a)


def solution(mesh):
    in_specs = (P("rows", "batch"), P("batch", None))
    out_specs = P(("rows", "batch"), None)
    return jax.shard_map(
        on_device, mesh=mesh, in_specs=in_specs, out_specs=out_specs, check_vma=False
    )
```

```python
import functools

import jax
import jax.numpy as jnp
from jax import lax
from jax.experimental import pallas as pl
from jax.experimental.pallas import tpu as pltpu
from jax.sharding import PartitionSpec as P

NB = 128
GROUPS = 8
RING = 4
CHIPS = 64
ORDERS = (("x", "y", "z"), ("y", "z", "x"), ("z", "x", "y"))
UNITS = (24, 24, 16)
HIGHEST = lax.Precision.HIGHEST
VMEM_SPEC = pl.BlockSpec(memory_space=pltpu.VMEM)
F32, BF16 = jnp.float32, jnp.bfloat16
NN, NT, TN = ((1,), (0,)), ((1,), (1,)), ((0,), (0,))


def dot_f32(left, right, dims):
    return lax.dot_general(
        left, right, (dims, ((), ())), precision=HIGHEST, preferred_element_type=F32
    )


def dot_low(left, right, dims):
    return lax.dot_general(left, right, (dims, ((), ())), preferred_element_type=F32)


def split(value):
    high = value.astype(BF16)
    return high, (value - high.astype(F32)).astype(BF16)


def stack(value):
    return jnp.concatenate(split(value), axis=0)


def fold(value):
    half = value.shape[0] // 2
    return value[:half] + value[half:]


def span(start, size, unit):
    return pl.ds(pl.multiple_of(start, unit), size)


def position():
    rows, batch = lax.axis_index("rows"), lax.axis_index("batch")
    return {
        "x": rows // 2 % 4,
        "y": batch % 4,
        "z": batch // 4 * 2 + rows // 8,
        "core": rows % 2,
    }


def device_at(pos):
    return {
        "rows": pos["z"] % 2 * 8 + pos["x"] * 2 + pos["core"],
        "batch": pos["z"] // 2 * 4 + pos["y"],
    }


def ring_peer(pos, axis, distance):
    there = dict(pos)
    there[axis] = (pos[axis] + distance) % RING
    return there


def sibling(pos):
    there = dict(pos)
    there["core"] = 1 - pos["core"]
    return there


def greet(peers):
    barrier = pltpu.get_barrier_semaphore()
    for peer in peers:
        pl.semaphore_signal(
            barrier, inc=1, device_id=device_at(peer), device_id_type=pl.DeviceIdType.MESH
        )
    pl.semaphore_wait(barrier, len(peers))


class Copies:
    def __init__(self, send_sem, recv_sem):
        self.send_sem, self.recv_sem = send_sem, recv_sem

    def copy(self, index, src, dst, peer):
        return pltpu.make_async_remote_copy(
            src_ref=src, dst_ref=dst,
            send_sem=self.send_sem.at[index], recv_sem=self.recv_sem.at[index],
            device_id=device_at(peer), device_id_type=pl.DeviceIdType.MESH,
        )


def batch_partners(pos, batch, count):
    partners = []
    for distance in range(1, count):
        other = (batch + distance) % count
        there = dict(pos)
        there["y"] = other % 4
        there["z"] = other // 4 * 2 + pos["z"] % 2
        partners.append(there)
    return partners


def exchange(
    pos, bases_ref, turned, a_ref, q_ref, energy_ref, e_send, e_recv, copies, own_sem
):
    core, x = pos["core"], pos["x"]
    batch = lax.axis_index("batch")
    count = lax.axis_size("batch")
    height = bases_ref.shape[0] // count
    width = bases_ref.shape[1]
    quarter = 64
    partners = batch_partners(pos, batch, count)
    x_peers = [ring_peer(pos, "x", d) for d in (1, 2, 3)]
    made = []

    def start(src, dst, peer):
        copy = copies.copy(len(made), src, dst, peer)
        copy.start()
        made.append(copy)
        return copy

    own_rows = span(core * height, height, 16)
    mine = span(x * quarter, quarter, 8)
    turned_rows = span(core * 256 + x * quarter, quarter, 8)

    def columns(which):
        return span(which * width, width, 128)

    def block_rows(which):
        return span(which * height, height, 16)

    def piece(which, half):
        return q_ref.at[which * 2 + half, mine, :]

    own_start = []
    for half in range(2):
        own = pltpu.make_async_copy(
            turned.at[turned_rows, half * 128:(half + 1) * 128], piece(batch, half),
            own_sem.at[half],
        )
        own.start()
        own_start.append(own)
    start_in = [
        [start(turned.at[turned_rows, half * 128:(half + 1) * 128], piece(batch, half), there)
         for half in range(2)]
        for there in partners
    ]
    x_in = [
        start(turned.at[turned_rows, half * 128:(half + 1) * 128], piece(batch, half), there)
        for half in range(2) for there in x_peers
    ]
    block_in = [
        start(bases_ref.at[block_rows((batch + d) % count), :],
              a_ref.at[own_rows, columns(batch)], there)
        for d, there in enumerate(partners, 1)
    ]
    own_block = pltpu.make_async_copy(
        bases_ref.at[block_rows(batch), :], a_ref.at[own_rows, columns(batch)], own_sem.at[2]
    )
    own_block.start()
    aside = [
        start(bases_ref.at[block_rows(batch), :], a_ref.at[own_rows, columns(batch)],
              sibling(pos))
    ]

    def add_square(step, total):
        value = bases_ref[span(step * 64, 64, 64), :].astype(F32)
        value = value * value
        return total + jnp.sum(value.reshape(8, 8, 2 * 128), axis=0)

    total = lax.fori_loop(
        0, bases_ref.shape[0] // 64, add_square, jnp.zeros((8, 2 * 128), F32)
    )
    total = total[:, :128] + total[:, 128:]

    for distance, pair in enumerate(start_in, 1):
        for copy in pair:
            copy.wait_recv()
        other = (batch + count - distance) % count
        block = q_ref.at[span(other * 2, 2, 2), mine, :]
        x_in += [start(block, block, there) for there in x_peers]
    for copy in own_start:
        copy.wait()
    rings = [[ring_peer(pos, axis, d) for d in (1, 2, 3)] for axis in "xyz"]
    for stage, peers in enumerate(rings + [[sibling(pos)]]):
        e_send[stage] = total
        incoming = [
            start(e_send.at[stage], e_recv.at[stage, slot], there)
            for slot, there in enumerate(peers)
        ]
        for slot, copy in enumerate(incoming):
            copy.wait_recv()
            total = total + e_recv[stage, slot]
    energy_ref[...] = jnp.broadcast_to(jnp.sum(total, keepdims=True), energy_ref.shape)
    for distance, copy in enumerate(block_in, 1):
        copy.wait_recv()
        other = (batch + count - distance) % count
        block = a_ref.at[own_rows, columns(other)]
        aside.append(start(block, block, sibling(pos)))
    own_block.wait()
    for copy in x_in + aside:
        copy.wait_recv()
    for copy in made:
        copy.wait_send()


EXCHANGE_COPIES = 14 + 6 + 7 + 1 + 21 + 10 + 7


class Reduction:
    def __init__(self, pos, part, work, out, slots, copies):
        self.pos, self.part, self.work, self.out = pos, part, work, out
        self.slots, self.copies = slots, copies
        self.base = [CHIPS * sum(UNITS[:k]) for k in range(3)]

    def axis(self, k, stage):
        return ORDERS[k][stage]

    def size(self, k, stage):
        return (16, 4, 1)[stage] * UNITS[k]

    def origin(self, k, depth):
        start = self.base[k]
        for stage in range(depth):
            start = start + self.pos[self.axis(k, stage)] * self.size(k, stage)
        return start

    def peer(self, k, stage, d):
        return ring_peer(self.pos, self.axis(k, stage), d)

    def sum_copy(self, k, stage, d):
        size = self.size(k, stage)
        source = self.part if stage == 0 else self.work
        target = (self.pos[self.axis(k, stage)] + d) % RING
        return self.copies.copy(
            9 * k + 3 * stage + d - 1,
            source.at[span(self.origin(k, stage) + target * size, size, 8), :],
            self.slots[3 * k + stage].at[d - 1],
            self.peer(k, stage, d),
        )

    def gather_copy(self, k, stage, d):
        block = self.block(self.origin(k, stage + 1), self.size(k, stage))
        return self.copies.copy(27 + 9 * k + 3 * stage + d - 1, block, block, self.peer(k, stage, d))

    def block(self, start, size):
        return self.out.at[self.pos["core"], span(start, size, 8), :]

    def aside_copy(self, k, d):
        size = self.size(k, 0)
        sender = (self.pos[self.axis(k, 0)] + RING - d) % RING
        block = self.block(self.base[k] + sender * size, size)
        return self.copies.copy(54 + 4 * k + d, block, block, sibling(self.pos))

    def start(self, k):
        for d in (1, 2, 3):
            self.sum_copy(k, 0, d).start()

    def step(self, number):
        for k in range(3):
            if number < 3:
                stage = number
                for d in (1, 2, 3):
                    self.sum_copy(k, stage, d).wait_recv()
                here = span(self.origin(k, stage + 1), self.size(k, stage), 8)
                source = self.part if stage == 0 else self.work
                slot = self.slots[3 * k + stage]
                value = source[here, :] + slot[0] + slot[1] + slot[2]
                if stage < 2:
                    self.work[here, :] = value
                    for d in (1, 2, 3):
                        self.sum_copy(k, stage + 1, d).start()
                else:
                    self.out[self.pos["core"], here, :] = value
                    for d in (1, 2, 3):
                        self.gather_copy(k, 2, d).start()
            else:
                stage = 5 - number
                for d in (1, 2, 3):
                    self.gather_copy(k, stage, d).wait_recv()
                    if stage == 0:
                        self.aside_copy(k, d).start()
                if stage:
                    for d in (1, 2, 3):
                        self.gather_copy(k, stage - 1, d).start()
                if stage == 1:
                    self.aside_copy(k, 0).start()

    def finish(self):
        for k in range(3):
            for d in range(4):
                self.aside_copy(k, d).wait()
            for d in (1, 2, 3):
                for stage in range(3):
                    self.sum_copy(k, stage, d).wait_send()
                    self.gather_copy(k, stage, d).wait_send()


REDUCE_COPIES = 27 + 27 + 12


def apply_gram(a_ref, q_block, scale, part, reduction):
    chunks = part.shape[0] // 256
    q = jnp.concatenate([q_block(chunk) for chunk in range(chunks)], axis=1)
    inner = stack(fold(dot_low(stack(q), a_ref[...], NT)))
    ready = 0
    for block in range(chunks // 2):
        value = fold(dot_low(inner, a_ref[:, block * 256:(block + 1) * 256], NN))
        for half in range(2):
            chunk = 2 * block + half
            part[chunk * 256:(chunk + 1) * 256, :] = (
                value[:, half * 128:(half + 1) * 128] * scale
                + q_block(chunk) * (1.0 / CHIPS))
        while ready < 3 and CHIPS * sum(UNITS[:ready + 1]) <= (block + 1) * 512:
            reduction.start(ready)
            ready += 1


def factor_block(aug, work):
    row = lax.broadcasted_iota(jnp.int32, (8, NB), 0)
    height = 8 * GROUPS
    for panel in range(NB // height):
        low = height * panel
        left = [aug[low + 8 * g:low + 8 * g + 8, :NB] for g in range(GROUPS)]
        right = [aug[low + 8 * g:low + 8 * g + 8, NB:] for g in range(GROUPS)]
        for s in range(GROUPS):
            rest = range(s, GROUPS)
            lane = low + 8 * s
            cols = {
                (g, k): jnp.broadcast_to(left[g][:, lane + k:lane + k + 1], (8, NB))
                for g in rest for k in range(8)
            }
            pivots = jnp.zeros((8, NB), F32)
            for k in range(8):
                pivot = jnp.broadcast_to(cols[s, k][k:k + 1, :], (8, NB))
                inverse = 1.0 / pivot
                pivots = jnp.where(row == k, pivot, pivots)
                mult = {g: cols[g, k] * inverse for g in rest}
                mult[s] = jnp.where(row > k, mult[s], 0.0)
                for j in range(k + 1, 8):
                    value = jnp.broadcast_to(cols[s, j][k:k + 1, :], (8, NB))
                    for g in rest:
                        cols[g, j] = cols[g, j] - mult[g] * value
                left_row = jnp.broadcast_to(left[s][k:k + 1, :], (8, NB))
                right_row = jnp.broadcast_to(right[s][k:k + 1, :], (8, NB))
                for g in rest:
                    left[g] = left[g] - mult[g] * left_row
                    right[g] = right[g] - mult[g] * right_row
            scale = lax.rsqrt(pivots)
            work[lane:lane + 8, :NB] = left[s] * scale
            work[lane:lane + 8, NB:] = right[s] * scale
        if low + height < NB:
            rows = work[low:low + height, :]
            aug[low + height:, :] = (
                aug[low + height:, :] - dot_f32(rows[:, :NB], rows, TN)[low + height:, :])


def inverse_factor(z_ref, rest, lower, aug, work, hooks=()):
    n = rest.shape[0]
    blocks = n // NB
    z_ref[...] = jnp.zeros_like(z_ref)
    row = lax.broadcasted_iota(jnp.int32, (NB, NB), 0)
    col = lax.broadcasted_iota(jnp.int32, (NB, NB), 1)

    @pl.loop(0, blocks)
    def _(j):
        here = span(j * NB, NB, NB)
        aug[:, :NB] = rest[here, here]
        aug[:, NB:] = jnp.where(row == col, 1.0, 0.0)
        factor_block(aug, work)
        for block in range(blocks):
            @pl.when(j == block)
            def _():
                low, high = block * NB, (block + 1) * NB
                inverse = jnp.where(row >= col, work[:, NB:], 0.0)
                z_ref[low:high, low:high] = inverse
                if high < n:
                    column = dot_f32(rest[high:, low:high], inverse, NT)
                    lower[high:, low:high] = column
                    rest[high:, high:] = rest[high:, high:] - dot_f32(column, column, NT)
                if low:
                    z_ref[low:high, :low] = -dot_f32(
                        inverse, dot_f32(lower[low:high, :low], z_ref[:low, :low], NN), NN)
                if block < len(hooks):
                    for hook in hooks[block]:
                        hook()


def whole_kernel(bases_ref, start_ref, modes_ref, *scratch):
    (turned, a_ref, q_ref, energy, e_send, e_recv, part, work, first, second, lifted,
     z_ref, rest, lower, aug, factor_work) = scratch[:16]
    slots = scratch[16:34]
    sems = scratch[34:40]
    own_sem = scratch[40]
    pos = position()
    core = pos["core"]
    turned[...] = start_ref[...].T
    peers = batch_partners(pos, lax.axis_index("batch"), lax.axis_size("batch"))
    peers += [ring_peer(pos, "x", d) for d in (1, 2, 3)]
    peers += [ring_peer(pos, "z", d) for d in (1, 3)] + [sibling(pos)]
    greet(peers)
    exchange(
        pos, bases_ref, turned, a_ref, q_ref, energy, e_send, e_recv,
        Copies(sems[0], sems[1]), own_sem,
    )
    n, all_columns = lifted.shape
    chunks = all_columns // NB
    scale = all_columns / energy[0:1, :]

    reduction = Reduction(pos, part.at[0], work.at[0], first, slots[:9], Copies(*sems[2:4]))
    apply_gram(a_ref, lambda chunk: q_ref[chunk], scale, part.at[0], reduction)
    for number in range(6):
        reduction.step(number)
    reduction.finish()

    reduction = Reduction(pos, part.at[1], work.at[1], second, slots[9:], Copies(*sems[4:]))
    apply_gram(
        a_ref, lambda chunk: first[core, chunk * 256:(chunk + 1) * 256, :], scale,
        part.at[1], reduction,
    )

    def side(ref, half):
        return jnp.concatenate(
            [ref[half, chunk * 256:(chunk + 1) * 256, :] for chunk in range(chunks)], axis=1)

    low = jnp.concatenate([side(first, half).astype(BF16) for half in range(2)], axis=0)
    rest[...] = dot_low(low, low, NT)
    step = [functools.partial(reduction.step, number) for number in range(6)]
    inverse_factor(
        z_ref, rest, lower, aug, factor_work, [[], step[:1], step[1:2], step[2:4]])
    step[4]()
    step[5]()
    reduction.finish()

    def times_factor(value_high, value_low, rows):
        z_stack = stack(z_ref[rows, :rows.stop])
        z_high = z_stack[:rows.stop - rows.start]
        return (fold(dot_low(z_stack, value_high[:rows.stop], NN))
                + dot_low(z_high, value_low[:rows.stop], NN))

    halves = [slice(0, n // 2), slice(n // 2, n)]
    blocks = 4
    width = all_columns // blocks
    rest[...] = jnp.zeros_like(rest)
    for block in range(blocks):
        value = jnp.concatenate(
            [jnp.concatenate(
                [second[half, chunk * 256:(chunk + 1) * 256, :]
                 for chunk in range(block * chunks // blocks, (block + 1) * chunks // blocks)],
                axis=1) for half in range(2)], axis=0)
        value_high, value_low = split(value)
        value = jnp.concatenate(
            [times_factor(value_high, value_low, rows) for rows in halves], axis=0)
        lifted[:, block * width:(block + 1) * width] = value
    both = stack(lifted[...])
    both = dot_low(both, both[:n], NT)
    rest[...] = both[:n] + both[n:] + both[n:].T
    inverse_factor(z_ref, rest, lower, aug, factor_work)

    height = modes_ref.shape[0]
    own_rows = span(core * height, height, 16)
    total = jnp.zeros(modes_ref.shape, F32)
    for block in range(blocks):
        here = slice(block * width, (block + 1) * width)
        value_high, value_low = split(lifted[:, here])
        q_low = jnp.concatenate(
            [times_factor(value_high, value_low, rows) for rows in halves], axis=0
        ).astype(BF16)
        total = total + dot_low(a_ref[own_rows, here], q_low, NT)
    modes_ref[...] = total.astype(BF16)


def on_device(bases, start):
    count = lax.axis_size("batch")
    width, n = start.shape
    all_columns = width * count
    height = bases.shape[0] // count
    flat = all_columns * n // 2 // 128
    sems = lambda number: [pltpu.SemaphoreType.DMA((number,))] * 2
    slots = [pltpu.VMEM((3, size * u, 128), F32) for u in UNITS for size in (16, 4, 1)]
    return pl.pallas_call(
        whole_kernel,
        out_shape=jax.ShapeDtypeStruct((height, n), BF16),
        in_specs=[VMEM_SPEC] * 2,
        out_specs=VMEM_SPEC,
        scratch_shapes=[
            pltpu.VMEM((n, width), F32),
            pltpu.VMEM((2 * height, all_columns), BF16),
            pltpu.VMEM((flat // 256, 256, 128), F32),
            pltpu.VMEM((8, 128), F32),
            pltpu.VMEM((4, 8, 128), F32),
            pltpu.VMEM((4, 3, 8, 128), F32),
            pltpu.VMEM((2, flat, 128), F32),
            pltpu.VMEM((2, flat, 128), F32),
            pltpu.VMEM((2, flat, 128), F32),
            pltpu.VMEM((2, flat, 128), F32),
            pltpu.VMEM((n, all_columns), F32),
            pltpu.VMEM((n, n), F32),
            pltpu.VMEM((n, n), F32),
            pltpu.VMEM((n, n), F32),
            pltpu.VMEM((NB, 2 * NB), F32),
            pltpu.VMEM((NB, 2 * NB), F32),
            *slots, *slots,
            *sems(EXCHANGE_COPIES), *sems(REDUCE_COPIES), *sems(REDUCE_COPIES),
            pltpu.SemaphoreType.DMA((3,)),
        ],
        compiler_params=pltpu.CompilerParams(
            collective_id=0, has_side_effects=True, vmem_limit_bytes=66_000_000
        ),
    )(bases, start)


def solution(mesh):
    in_specs = (P("rows", "batch"), P("batch", None))
    out_specs = P(("rows", "batch"), None)
    return jax.shard_map(
        on_device, mesh=mesh, in_specs=in_specs, out_specs=out_specs, check_vma=False
    )
```

```python
import functools

import jax
import jax.numpy as jnp
from jax import lax
from jax.experimental import pallas as pl
from jax.experimental.pallas import tpu as pltpu
from jax.sharding import PartitionSpec as P

NB = 128
GROUPS = 8
RING = 4
CHIPS = 64
ORDERS = (("x", "y", "z"), ("y", "z", "x"), ("z", "x", "y")) * 2
UNITS = (16, 8, 8, 8, 16, 8)
COLOURS = len(UNITS)
HIGHEST = lax.Precision.HIGHEST
VMEM_SPEC = pl.BlockSpec(memory_space=pltpu.VMEM)
F32, BF16 = jnp.float32, jnp.bfloat16
NN, NT, TN = ((1,), (0,)), ((1,), (1,)), ((0,), (0,))


def dot_f32(left, right, dims):
    return lax.dot_general(
        left, right, (dims, ((), ())), precision=HIGHEST, preferred_element_type=F32
    )


def dot_low(left, right, dims):
    return lax.dot_general(left, right, (dims, ((), ())), preferred_element_type=F32)


def split(value):
    high = value.astype(BF16)
    return high, (value - high.astype(F32)).astype(BF16)


def stack(value):
    return jnp.concatenate(split(value), axis=0)


def fold(value):
    half = value.shape[0] // 2
    return value[:half] + value[half:]


def span(start, size, unit):
    return pl.ds(pl.multiple_of(start, unit), size)


def position():
    rows, batch = lax.axis_index("rows"), lax.axis_index("batch")
    return {
        "x": rows // 2 % 4,
        "y": batch % 4,
        "z": batch // 4 * 2 + rows // 8,
        "core": rows % 2,
    }


def device_at(pos):
    return {
        "rows": pos["z"] % 2 * 8 + pos["x"] * 2 + pos["core"],
        "batch": pos["z"] // 2 * 4 + pos["y"],
    }


def ring_peer(pos, axis, distance):
    there = dict(pos)
    there[axis] = (pos[axis] + distance) % RING
    return there


def sibling(pos):
    there = dict(pos)
    there["core"] = 1 - pos["core"]
    return there


def greet(peers):
    barrier = pltpu.get_barrier_semaphore()
    for peer in peers:
        pl.semaphore_signal(
            barrier, inc=1, device_id=device_at(peer), device_id_type=pl.DeviceIdType.MESH
        )
    pl.semaphore_wait(barrier, len(peers))


class Copies:
    def __init__(self, send_sem, recv_sem):
        self.send_sem, self.recv_sem = send_sem, recv_sem

    def copy(self, index, src, dst, peer):
        return pltpu.make_async_remote_copy(
            src_ref=src, dst_ref=dst,
            send_sem=self.send_sem.at[index], recv_sem=self.recv_sem.at[index],
            device_id=device_at(peer), device_id_type=pl.DeviceIdType.MESH,
        )


def batch_partners(pos, batch, count):
    partners = []
    for distance in range(1, count):
        other = (batch + distance) % count
        there = dict(pos)
        there["y"] = other % 4
        there["z"] = other // 4 * 2 + pos["z"] % 2
        partners.append(there)
    return partners


def exchange(
    pos, bases_ref, turned, a_ref, q_ref, energy_ref, e_send, e_recv, copies, own_sem
):
    core, x = pos["core"], pos["x"]
    batch = lax.axis_index("batch")
    count = lax.axis_size("batch")
    height = bases_ref.shape[0] // count
    width = bases_ref.shape[1]
    quarter = 64
    partners = batch_partners(pos, batch, count)
    x_peers = [ring_peer(pos, "x", d) for d in (1, 2, 3)]
    made = []

    def start(src, dst, peer):
        copy = copies.copy(len(made), src, dst, peer)
        copy.start()
        made.append(copy)
        return copy

    own_rows = span(core * height, height, 16)
    mine = span(x * quarter, quarter, 8)
    turned_rows = span(core * 256 + x * quarter, quarter, 8)

    def columns(which):
        return span(which * width, width, 128)

    def block_rows(which):
        return span(which * height, height, 16)

    def piece(which, half):
        return q_ref.at[which * 2 + half, mine, :]

    own_start = []
    for half in range(2):
        own = pltpu.make_async_copy(
            turned.at[turned_rows, half * 128:(half + 1) * 128], piece(batch, half),
            own_sem.at[half],
        )
        own.start()
        own_start.append(own)
    start_in = [
        [start(turned.at[turned_rows, half * 128:(half + 1) * 128], piece(batch, half), there)
         for half in range(2)]
        for there in partners
    ]
    x_in = [
        start(turned.at[turned_rows, half * 128:(half + 1) * 128], piece(batch, half), there)
        for half in range(2) for there in x_peers
    ]
    block_in = [
        start(bases_ref.at[block_rows((batch + d) % count), :],
              a_ref.at[own_rows, columns(batch)], there)
        for d, there in enumerate(partners, 1)
    ]
    own_block = pltpu.make_async_copy(
        bases_ref.at[block_rows(batch), :], a_ref.at[own_rows, columns(batch)], own_sem.at[2]
    )
    own_block.start()
    aside = [
        start(bases_ref.at[block_rows(batch), :], a_ref.at[own_rows, columns(batch)],
              sibling(pos))
    ]

    def add_square(step, total):
        value = bases_ref[span(step * 64, 64, 64), :].astype(F32)
        value = value * value
        return total + jnp.sum(value.reshape(8, 8, 2 * 128), axis=0)

    total = lax.fori_loop(
        0, bases_ref.shape[0] // 64, add_square, jnp.zeros((8, 2 * 128), F32)
    )
    total = total[:, :128] + total[:, 128:]

    rings = [[ring_peer(pos, axis, d) for d in (1, 2, 3)] for axis in "xyz"]
    rings.append([sibling(pos)])

    def send_energy(stage, total):
        e_send[stage] = total
        return [
            start(e_send.at[stage], e_recv.at[stage, slot], there)
            for slot, there in enumerate(rings[stage])
        ]

    def add_energy(stage, incoming, total):
        for slot, copy in enumerate(incoming):
            copy.wait_recv()
            total = total + e_recv[stage, slot]
        return total

    incoming = send_energy(0, total)
    for distance, pair in enumerate(start_in, 1):
        for copy in pair:
            copy.wait_recv()
        other = (batch + count - distance) % count
        block = q_ref.at[span(other * 2, 2, 2), mine, :]
        x_in += [start(block, block, there) for there in x_peers]
    for copy in own_start:
        copy.wait()
    own_block.wait()
    stage = 0
    for distance, copy in enumerate(block_in, 1):
        if distance % 2:
            total = add_energy(stage, incoming, total)
            stage += 1
            if stage < 4:
                incoming = send_energy(stage, total)
        copy.wait_recv()
        other = (batch + count - distance) % count
        block = a_ref.at[own_rows, columns(other)]
        aside.append(start(block, block, sibling(pos)))
    energy_ref[...] = jnp.broadcast_to(jnp.sum(total, keepdims=True), energy_ref.shape)
    for copy in x_in + aside:
        copy.wait_recv()
    for copy in made:
        copy.wait_send()


EXCHANGE_COPIES = 14 + 6 + 7 + 1 + 21 + 10 + 7


class Reduction:
    def __init__(self, pos, part, work, out, slots, copies):
        self.pos, self.part, self.work, self.out = pos, part, work, out
        self.slots, self.copies = slots, copies
        self.base = [CHIPS * sum(UNITS[:k]) for k in range(COLOURS)]

    def axis(self, k, stage):
        return ORDERS[k][stage]

    def size(self, k, stage):
        return (16, 4, 1)[stage] * UNITS[k]

    def origin(self, k, depth):
        start = self.base[k]
        for stage in range(depth):
            start = start + self.pos[self.axis(k, stage)] * self.size(k, stage)
        return start

    def peer(self, k, stage, d):
        return ring_peer(self.pos, self.axis(k, stage), d)

    def sum_copy(self, k, stage, d):
        size = self.size(k, stage)
        source = self.part if stage == 0 else self.work
        target = (self.pos[self.axis(k, stage)] + d) % RING
        return self.copies.copy(
            9 * k + 3 * stage + d - 1,
            source.at[span(self.origin(k, stage) + target * size, size, 8), :],
            self.slots[3 * k + stage].at[d - 1],
            self.peer(k, stage, d),
        )

    def gather_copy(self, k, stage, d):
        block = self.block(self.origin(k, stage + 1), self.size(k, stage))
        return self.copies.copy(9 * COLOURS + 9 * k + 3 * stage + d - 1, block, block, self.peer(k, stage, d))

    def block(self, start, size):
        return self.out.at[self.pos["core"], span(start, size, 8), :]

    def aside_copy(self, k, d):
        size = self.size(k, 0)
        sender = (self.pos[self.axis(k, 0)] + RING - d) % RING
        block = self.block(self.base[k] + sender * size, size)
        return self.copies.copy(18 * COLOURS + 4 * k + d, block, block, sibling(self.pos))

    def start(self, k):
        for d in (1, 2, 3):
            self.sum_copy(k, 0, d).start()

    def step(self, number, colours=range(COLOURS)):
        for k in colours:
            if number < 3:
                stage = number
                for d in (1, 2, 3):
                    self.sum_copy(k, stage, d).wait_recv()
                here = span(self.origin(k, stage + 1), self.size(k, stage), 8)
                source = self.part if stage == 0 else self.work
                slot = self.slots[3 * k + stage]
                value = source[here, :] + slot[0] + slot[1] + slot[2]
                if stage < 2:
                    self.work[here, :] = value
                    for d in (1, 2, 3):
                        self.sum_copy(k, stage + 1, d).start()
                else:
                    self.out[self.pos["core"], here, :] = value
                    for d in (1, 2, 3):
                        self.gather_copy(k, 2, d).start()
            else:
                stage = 5 - number
                for d in (1, 2, 3):
                    self.gather_copy(k, stage, d).wait_recv()
                    if stage == 0:
                        self.aside_copy(k, d).start()
                if stage:
                    for d in (1, 2, 3):
                        self.gather_copy(k, stage - 1, d).start()
                if stage == 1:
                    self.aside_copy(k, 0).start()

    def join(self):
        for k in range(COLOURS):
            for d in range(4):
                self.aside_copy(k, d).wait_recv()

    def finish(self):
        for k in range(COLOURS):
            for d in range(4):
                self.aside_copy(k, d).wait_send()
            for d in (1, 2, 3):
                for stage in range(3):
                    self.sum_copy(k, stage, d).wait_send()
                    self.gather_copy(k, stage, d).wait_send()


REDUCE_COPIES = (9 + 9 + 4) * COLOURS


def apply_gram(a_ref, q_block, scale, part, reduction):
    chunks = part.shape[0] // 256
    q = jnp.concatenate([q_block(chunk) for chunk in range(chunks)], axis=1)
    inner = stack(fold(dot_low(stack(q), a_ref[...], NT)))
    ready = 0
    for block in range(chunks // 2):
        value = fold(dot_low(inner, a_ref[:, block * 256:(block + 1) * 256], NN))
        for half in range(2):
            chunk = 2 * block + half
            part[chunk * 256:(chunk + 1) * 256, :] = (
                value[:, half * 128:(half + 1) * 128] * scale
                + q_block(chunk) * (1.0 / CHIPS))
        while ready < COLOURS and CHIPS * sum(UNITS[:ready + 1]) <= (block + 1) * 512:
            reduction.start(ready)
            ready += 1


def factor_block(aug, work, between=lambda: None):
    row = lax.broadcasted_iota(jnp.int32, (8, NB), 0)
    height = 8 * GROUPS
    for panel in range(NB // height):
        low = height * panel
        left = [aug[low + 8 * g:low + 8 * g + 8, :NB] for g in range(GROUPS)]
        right = [aug[low + 8 * g:low + 8 * g + 8, NB:] for g in range(GROUPS)]
        for s in range(GROUPS):
            rest = range(s, GROUPS)
            lane = low + 8 * s
            cols = {
                (g, k): jnp.broadcast_to(left[g][:, lane + k:lane + k + 1], (8, NB))
                for g in rest for k in range(8)
            }
            pivots = jnp.zeros((8, NB), F32)
            for k in range(8):
                pivot = jnp.broadcast_to(cols[s, k][k:k + 1, :], (8, NB))
                inverse = 1.0 / pivot
                pivots = jnp.where(row == k, pivot, pivots)
                mult = {g: cols[g, k] * inverse for g in rest}
                mult[s] = jnp.where(row > k, mult[s], 0.0)
                for j in range(k + 1, 8):
                    value = jnp.broadcast_to(cols[s, j][k:k + 1, :], (8, NB))
                    for g in rest:
                        cols[g, j] = cols[g, j] - mult[g] * value
                left_row = jnp.broadcast_to(left[s][k:k + 1, :], (8, NB))
                right_row = jnp.broadcast_to(right[s][k:k + 1, :], (8, NB))
                for g in rest:
                    left[g] = left[g] - mult[g] * left_row
                    right[g] = right[g] - mult[g] * right_row
            scale = lax.rsqrt(pivots)
            work[lane:lane + 8, :NB] = left[s] * scale
            work[lane:lane + 8, NB:] = right[s] * scale
        if low + height < NB:
            rows = work[low:low + height, :]
            aug[low + height:, :] = (
                aug[low + height:, :] - dot_f32(rows[:, :NB], rows, TN)[low + height:, :])
            between()


def inverse_factor(z_ref, rest, lower, aug, work, hooks={}):
    n = rest.shape[0]
    blocks = n // NB
    z_ref[...] = jnp.zeros_like(z_ref)
    row = lax.broadcasted_iota(jnp.int32, (NB, NB), 0)
    col = lax.broadcasted_iota(jnp.int32, (NB, NB), 1)

    @pl.loop(0, blocks)
    def _(j):
        here = span(j * NB, NB, NB)
        aug[:, :NB] = rest[here, here]
        aug[:, NB:] = jnp.where(row == col, 1.0, 0.0)

        def between():
            for block in range(blocks):
                if (block, 0) in hooks:
                    pl.when(j == block)(hooks[block, 0])

        factor_block(aug, work, between)
        for block in range(blocks):
            @pl.when(j == block)
            def _():
                low, high = block * NB, (block + 1) * NB
                inverse = jnp.where(row >= col, work[:, NB:], 0.0)
                z_ref[low:high, low:high] = inverse
                if high < n:
                    column = dot_f32(rest[high:, low:high], inverse, NT)
                    lower[high:, low:high] = column
                    rest[high:, high:] = rest[high:, high:] - dot_f32(column, column, NT)
                if low:
                    z_ref[low:high, :low] = -dot_f32(
                        inverse, dot_f32(lower[low:high, :low], z_ref[:low, :low], NN), NN)
                hooks.get((block, 1), lambda: None)()


def whole_kernel(bases_ref, start_ref, modes_ref, *scratch):
    (turned, a_ref, q_ref, energy, e_send, e_recv, part, work, first, second, lifted,
     z_ref, rest, lower, aug, factor_work) = scratch[:16]
    slots, sems, own_sem = scratch[16:-7], scratch[-7:-1], scratch[-1]
    pos = position()
    core = pos["core"]
    turned[...] = start_ref[...].T
    peers = batch_partners(pos, lax.axis_index("batch"), lax.axis_size("batch"))
    peers += [ring_peer(pos, "x", d) for d in (1, 2, 3)]
    peers += [ring_peer(pos, "z", d) for d in (1, 3)] + [sibling(pos)]
    greet(peers)
    exchange(
        pos, bases_ref, turned, a_ref, q_ref, energy, e_send, e_recv,
        Copies(sems[0], sems[1]), own_sem,
    )
    n, all_columns = lifted.shape
    chunks = all_columns // NB
    scale = all_columns / energy[0:1, :]

    reduction = Reduction(pos, part.at[0], work.at[0], first, slots[:3 * COLOURS], Copies(*sems[2:4]))
    early = reduction
    apply_gram(a_ref, lambda chunk: q_ref[chunk], scale, part.at[0], reduction)
    for number in range(6):
        reduction.step(number)

    reduction = Reduction(pos, part.at[1], work.at[1], second, slots[3 * COLOURS:], Copies(*sems[4:]))
    apply_gram(
        a_ref, lambda chunk: first[core, chunk * 256:(chunk + 1) * 256, :], scale,
        part.at[1], reduction,
    )

    def side(ref, half):
        return jnp.concatenate(
            [ref[half, chunk * 256:(chunk + 1) * 256, :] for chunk in range(chunks)], axis=1)

    early.join()
    low = jnp.concatenate([side(first, half).astype(BF16) for half in range(2)], axis=0)
    rest[...] = dot_low(low, low, NT)
    sets = [range(3), range(3, 6)]
    inverse_factor(
        z_ref, rest, lower, aug, factor_work,
        {(stage + 1, part): functools.partial(reduction.step, stage, sets[part])
         for stage in range(3) for part in range(2)},
    )
    for stage in (3, 4, 5):
        reduction.step(stage)
    reduction.join()

    def times_factor(value_high, value_low, rows):
        z_stack = stack(z_ref[rows, :rows.stop])
        z_high = z_stack[:rows.stop - rows.start]
        return (fold(dot_low(z_stack, value_high[:rows.stop], NN))
                + dot_low(z_high, value_low[:rows.stop], NN))

    halves = [slice(0, n // 2), slice(n // 2, n)]
    blocks = 4
    width = all_columns // blocks
    rest[...] = jnp.zeros_like(rest)
    for block in range(blocks):
        value = jnp.concatenate(
            [jnp.concatenate(
                [second[half, chunk * 256:(chunk + 1) * 256, :]
                 for chunk in range(block * chunks // blocks, (block + 1) * chunks // blocks)],
                axis=1) for half in range(2)], axis=0)
        value_high, value_low = split(value)
        value = jnp.concatenate(
            [times_factor(value_high, value_low, rows) for rows in halves], axis=0)
        lifted[:, block * width:(block + 1) * width] = value
    both = stack(lifted[...])
    both = dot_low(both, both[:n], NT)
    rest[...] = both[:n] + both[n:] + both[n:].T
    inverse_factor(z_ref, rest, lower, aug, factor_work)

    height = modes_ref.shape[0]
    own_rows = span(core * height, height, 16)
    total = jnp.zeros(modes_ref.shape, F32)
    for block in range(blocks):
        here = slice(block * width, (block + 1) * width)
        value_high, value_low = split(lifted[:, here])
        q_low = jnp.concatenate(
            [times_factor(value_high, value_low, rows) for rows in halves], axis=0
        ).astype(BF16)
        total = total + dot_low(a_ref[own_rows, here], q_low, NT)
    modes_ref[...] = total.astype(BF16)
    early.finish()
    reduction.finish()


def on_device(bases, start):
    count = lax.axis_size("batch")
    width, n = start.shape
    all_columns = width * count
    height = bases.shape[0] // count
    flat = all_columns * n // 2 // 128
    sems = lambda number: [pltpu.SemaphoreType.DMA((number,))] * 2
    slots = [pltpu.VMEM((3, size * u, 128), F32) for u in UNITS for size in (16, 4, 1)]
    return pl.pallas_call(
        whole_kernel,
        out_shape=jax.ShapeDtypeStruct((height, n), BF16),
        in_specs=[VMEM_SPEC] * 2,
        out_specs=VMEM_SPEC,
        scratch_shapes=[
            pltpu.VMEM((n, width), F32),
            pltpu.VMEM((2 * height, all_columns), BF16),
            pltpu.VMEM((flat // 256, 256, 128), F32),
            pltpu.VMEM((8, 128), F32),
            pltpu.VMEM((4, 8, 128), F32),
            pltpu.VMEM((4, 3, 8, 128), F32),
            pltpu.VMEM((2, flat, 128), F32),
            pltpu.VMEM((2, flat, 128), F32),
            pltpu.VMEM((2, flat, 128), F32),
            pltpu.VMEM((2, flat, 128), F32),
            pltpu.VMEM((n, all_columns), F32),
            pltpu.VMEM((n, n), F32),
            pltpu.VMEM((n, n), F32),
            pltpu.VMEM((n, n), F32),
            pltpu.VMEM((NB, 2 * NB), F32),
            pltpu.VMEM((NB, 2 * NB), F32),
            *slots, *slots,
            *sems(EXCHANGE_COPIES), *sems(REDUCE_COPIES), *sems(REDUCE_COPIES),
            pltpu.SemaphoreType.DMA((3,)),
        ],
        compiler_params=pltpu.CompilerParams(
            collective_id=0, has_side_effects=True, vmem_limit_bytes=66_000_000
        ),
    )(bases, start)


def solution(mesh):
    in_specs = (P("rows", "batch"), P("batch", None))
    out_specs = P(("rows", "batch"), None)
    return jax.shard_map(
        on_device, mesh=mesh, in_specs=in_specs, out_specs=out_specs, check_vma=False
    )
```

```python
import functools

import jax
import jax.numpy as jnp
from jax import lax
from jax.experimental import pallas as pl
from jax.experimental.pallas import tpu as pltpu
from jax.sharding import PartitionSpec as P

NB = 128
GROUPS = 8
RING = 4
CHIPS = 64
ORDERS = (("x", "y", "z"), ("y", "z", "x"), ("z", "x", "y")) * 2
UNITS = (16, 8, 8, 8, 16, 8)
COLOURS = len(UNITS)
HIGHEST = lax.Precision.HIGHEST
VMEM_SPEC = pl.BlockSpec(memory_space=pltpu.VMEM)
F32, BF16 = jnp.float32, jnp.bfloat16
NN, NT, TN = ((1,), (0,)), ((1,), (1,)), ((0,), (0,))


def dot_f32(left, right, dims):
    return lax.dot_general(
        left, right, (dims, ((), ())), precision=HIGHEST, preferred_element_type=F32
    )


def dot_low(left, right, dims):
    return lax.dot_general(left, right, (dims, ((), ())), preferred_element_type=F32)


def split(value):
    high = value.astype(BF16)
    return high, (value - high.astype(F32)).astype(BF16)


def stack(value):
    return jnp.concatenate(split(value), axis=0)


def fold(value):
    half = value.shape[0] // 2
    return value[:half] + value[half:]


def span(start, size, unit):
    return pl.ds(pl.multiple_of(start, unit), size)


def position():
    rows, batch = lax.axis_index("rows"), lax.axis_index("batch")
    return {
        "x": rows // 2 % 4,
        "y": batch % 4,
        "z": batch // 4 * 2 + rows // 8,
        "core": rows % 2,
    }


def device_at(pos):
    return {
        "rows": pos["z"] % 2 * 8 + pos["x"] * 2 + pos["core"],
        "batch": pos["z"] // 2 * 4 + pos["y"],
    }


def ring_peer(pos, axis, distance):
    there = dict(pos)
    there[axis] = (pos[axis] + distance) % RING
    return there


def sibling(pos):
    there = dict(pos)
    there["core"] = 1 - pos["core"]
    return there


def greet(peers, work):
    barrier = pltpu.get_barrier_semaphore()
    for peer in peers:
        pl.semaphore_signal(
            barrier, inc=1, device_id=device_at(peer), device_id_type=pl.DeviceIdType.MESH
        )
    work()
    pl.semaphore_wait(barrier, len(peers))


class Copies:
    def __init__(self, send_sem, recv_sem):
        self.send_sem, self.recv_sem = send_sem, recv_sem

    def copy(self, index, src, dst, peer):
        return pltpu.make_async_remote_copy(
            src_ref=src, dst_ref=dst,
            send_sem=self.send_sem.at[index], recv_sem=self.recv_sem.at[index],
            device_id=device_at(peer), device_id_type=pl.DeviceIdType.MESH,
        )


def batch_partners(pos, batch, count):
    partners = []
    for distance in range(1, count):
        other = (batch + distance) % count
        there = dict(pos)
        there["y"] = other % 4
        there["z"] = other // 4 * 2 + pos["z"] % 2
        partners.append(there)
    return partners


def exchange(pos, bases_ref, turned, a_ref, q_ref, energy, copies, own_sem):
    core, x = pos["core"], pos["x"]
    batch = lax.axis_index("batch")
    count = lax.axis_size("batch")
    height = bases_ref.shape[0] // count
    width = bases_ref.shape[1]
    quarter = 64
    partners = batch_partners(pos, batch, count)
    x_peers = [ring_peer(pos, "x", d) for d in (1, 2, 3)]
    made = []

    def start(src, dst, peer):
        copy = copies.copy(len(made), src, dst, peer)
        copy.start()
        made.append(copy)
        return copy

    own_rows = span(core * height, height, 16)
    mine = span(x * quarter, quarter, 8)
    turned_rows = span(core * 256 + x * quarter, quarter, 8)

    def columns(which):
        return span(which * width, width, 128)

    def block_rows(which):
        return span(which * height, height, 16)

    def piece(which, half):
        return q_ref.at[which * 2 + half, mine, :]

    own_start = []
    for half in range(2):
        own = pltpu.make_async_copy(
            turned.at[turned_rows, half * 128:(half + 1) * 128], piece(batch, half),
            own_sem.at[half],
        )
        own.start()
        own_start.append(own)
    start_in = [
        [start(turned.at[turned_rows, half * 128:(half + 1) * 128], piece(batch, half), there)
         for half in range(2)]
        for there in partners
    ]
    x_in = [
        start(turned.at[turned_rows, half * 128:(half + 1) * 128], piece(batch, half), there)
        for half in range(2) for there in x_peers
    ]
    block_in = [
        start(bases_ref.at[block_rows((batch + d) % count), :],
              a_ref.at[own_rows, columns(batch)], there)
        for d, there in enumerate(partners, 1)
    ]
    own_block = pltpu.make_async_copy(
        bases_ref.at[block_rows(batch), :], a_ref.at[own_rows, columns(batch)], own_sem.at[2]
    )
    own_block.start()
    aside = [
        start(bases_ref.at[block_rows(batch), :], a_ref.at[own_rows, columns(batch)],
              sibling(pos))
    ]

    def add_square(step, total):
        value = bases_ref[span(step * 64, 64, 64), :].astype(F32)
        value = value * value
        return total + jnp.sum(value.reshape(8, 8, 2 * 128), axis=0)

    total = lax.fori_loop(
        0, bases_ref.shape[0] // 64, add_square, jnp.zeros((8, 2 * 128), F32)
    )
    total = total[:, :128] + total[:, 128:]

    energy.begin(total)
    for distance, pair in enumerate(start_in, 1):
        for copy in pair:
            copy.wait_recv()
        other = (batch + count - distance) % count
        block = q_ref.at[span(other * 2, 2, 2), mine, :]
        x_in += [start(block, block, there) for there in x_peers]
    for copy in own_start:
        copy.wait()
    own_block.wait()
    for distance, copy in enumerate(block_in, 1):
        copy.wait_recv()
        other = (batch + count - distance) % count
        block = a_ref.at[own_rows, columns(other)]
        aside.append(start(block, block, sibling(pos)))
    for copy in x_in + aside:
        copy.wait_recv()
    for copy in made:
        copy.wait_send()


EXCHANGE_COPIES = 14 + 6 + 7 + 1 + 21 + 7


class Energy:
    def __init__(self, pos, sums, slots, copies):
        self.sums, self.slots, self.copies = sums, slots, copies
        self.rings = [[ring_peer(pos, axis, d) for d in (1, 2, 3)] for axis in "xyz"]
        self.rings.append([sibling(pos)])

    def copy(self, stage, slot):
        return self.copies.copy(
            3 * stage + slot, self.sums.at[stage], self.slots.at[stage, slot],
            self.rings[stage][slot],
        )

    def begin(self, total):
        self.sums[0] = total
        for slot in range(3):
            self.copy(0, slot).start()

    def step(self, stage):
        total = self.sums[stage]
        for slot in range(len(self.rings[stage])):
            self.copy(stage, slot).wait()
            total = total + self.slots[stage, slot]
        self.sums[stage + 1] = total
        if stage < 3:
            for slot in range(len(self.rings[stage + 1])):
                self.copy(stage + 1, slot).start()

    def value(self):
        return jnp.sum(self.sums[4], keepdims=True)


ENERGY_COPIES = 10


class Reduction:
    def __init__(self, pos, part, part_low, work, out, slots, copies, forward):
        self.pos, self.part, self.work, self.out = pos, part, work, out
        self.part_low, self.forward = part_low, forward
        self.slots, self.copies = slots, copies
        self.base = [CHIPS * sum(UNITS[:k]) for k in range(COLOURS)]

    def axis(self, k, stage):
        return ORDERS[k][stage]

    def size(self, k, stage):
        return (16, 4, 1)[stage] * UNITS[k]

    def origin(self, k, depth):
        start = self.base[k]
        for stage in range(depth):
            start = start + self.pos[self.axis(k, stage)] * self.size(k, stage)
        return start

    def peer(self, k, stage, d):
        return ring_peer(self.pos, self.axis(k, stage), d)

    def sum_copy(self, k, stage, d):
        size = self.size(k, stage)
        source = self.part_low if stage == 0 else self.work
        target = (self.pos[self.axis(k, stage)] + d) % RING
        return self.copies.copy(
            9 * k + 3 * stage + d - 1,
            source.at[span(self.origin(k, stage) + target * size, size, 8 if stage else 16), :],
            self.slots[3 * k + stage].at[d - 1],
            self.peer(k, stage, d),
        )

    def gather_copy(self, k, stage, d):
        block = self.block(self.origin(k, stage + 1), self.size(k, stage))
        return self.copies.copy(9 * COLOURS + 9 * k + 3 * stage + d - 1, block, block, self.peer(k, stage, d))

    def block(self, start, size):
        return self.out.at[self.pos["core"], span(start, size, 8), :]

    def aside_copy(self, k, d):
        size = self.size(k, 0)
        sender = (self.pos[self.axis(k, 0)] + RING - d) % RING
        block = self.block(self.base[k] + sender * size, size)
        return self.copies.copy(18 * COLOURS + 4 * k + d, block, block, sibling(self.pos))

    def start(self, k):
        for d in (1, 2, 3):
            self.sum_copy(k, 0, d).start()

    def step(self, number, colours=range(COLOURS)):
        for k in colours:
            if number < 3:
                stage = number
                for d in (1, 2, 3):
                    self.sum_copy(k, stage, d).wait_recv()
                here = span(self.origin(k, stage + 1), self.size(k, stage), 8)
                source = self.part if stage == 0 else self.work
                slot = self.slots[3 * k + stage]
                value = source[here, :]
                for d in range(3):
                    value = value + slot[d].astype(F32)
                if stage < 2:
                    self.work[here, :] = value
                    for d in (1, 2, 3):
                        self.sum_copy(k, stage + 1, d).start()
                else:
                    self.out[self.pos["core"], here, :] = value
                    for d in (1, 2, 3):
                        self.gather_copy(k, 2, d).start()
            else:
                stage = 5 - number
                for d in (1, 2, 3):
                    self.gather_copy(k, stage, d).wait_recv()
                    if stage == 0 and self.forward:
                        self.aside_copy(k, d).start()
                if stage:
                    for d in (1, 2, 3):
                        self.gather_copy(k, stage - 1, d).start()
                if stage == 1 and self.forward:
                    self.aside_copy(k, 0).start()

    def join(self):
        for k in range(COLOURS):
            for d in range(4):
                self.aside_copy(k, d).wait_recv()

    def finish(self):
        for k in range(COLOURS):
            if self.forward:
                for d in range(4):
                    self.aside_copy(k, d).wait_send()
            for d in (1, 2, 3):
                for stage in range(3):
                    self.sum_copy(k, stage, d).wait_send()
                    self.gather_copy(k, stage, d).wait_send()


REDUCE_COPIES = (9 + 9 + 4) * COLOURS


def apply_gram(a_ref, q_block, combine, reduction):
    chunks = a_ref.shape[1] // 128
    q = jnp.concatenate([q_block(chunk) for chunk in range(chunks)], axis=1)
    inner = stack(fold(dot_low(stack(q), a_ref[...], NT)))
    ready = 0
    for block in range(chunks // 2):
        value = fold(dot_low(inner, a_ref[:, block * 256:(block + 1) * 256], NN))
        for half in range(2):
            chunk = 2 * block + half
            share = combine(value[:, half * 128:(half + 1) * 128], chunk)
            here = slice(chunk * 256, (chunk + 1) * 256)
            reduction.part[here, :] = share
            reduction.part_low[here, :] = share.astype(BF16)
        while ready < COLOURS and CHIPS * sum(UNITS[:ready + 1]) <= (block + 1) * 512:
            reduction.start(ready)
            ready += 1


def factor_block(aug, work, between=lambda: None):
    row = lax.broadcasted_iota(jnp.int32, (8, NB), 0)
    height = 8 * GROUPS
    for panel in range(NB // height):
        low = height * panel
        left = [aug[low + 8 * g:low + 8 * g + 8, :NB] for g in range(GROUPS)]
        right = [aug[low + 8 * g:low + 8 * g + 8, NB:] for g in range(GROUPS)]
        for s in range(GROUPS):
            rest = range(s, GROUPS)
            lane = low + 8 * s
            cols = {
                (g, k): jnp.broadcast_to(left[g][:, lane + k:lane + k + 1], (8, NB))
                for g in rest for k in range(8)
            }
            pivots = jnp.zeros((8, NB), F32)
            for k in range(8):
                pivot = jnp.broadcast_to(cols[s, k][k:k + 1, :], (8, NB))
                inverse = 1.0 / pivot
                pivots = jnp.where(row == k, pivot, pivots)
                mult = {g: cols[g, k] * inverse for g in rest}
                mult[s] = jnp.where(row > k, mult[s], 0.0)
                for j in range(k + 1, 8):
                    value = jnp.broadcast_to(cols[s, j][k:k + 1, :], (8, NB))
                    for g in rest:
                        cols[g, j] = cols[g, j] - mult[g] * value
                left_row = jnp.broadcast_to(left[s][k:k + 1, :], (8, NB))
                right_row = jnp.broadcast_to(right[s][k:k + 1, :], (8, NB))
                for g in rest:
                    left[g] = left[g] - mult[g] * left_row
                    right[g] = right[g] - mult[g] * right_row
            scale = lax.rsqrt(pivots)
            work[lane:lane + 8, :NB] = left[s] * scale
            work[lane:lane + 8, NB:] = right[s] * scale
        if low + height < NB:
            rows = work[low:low + height, :]
            aug[low + height:, :] = (
                aug[low + height:, :] - dot_f32(rows[:, :NB], rows, TN)[low + height:, :])
            between()


def inverse_factor(z_ref, rest, lower, aug, work, hooks={}):
    n = rest.shape[0]
    blocks = n // NB
    z_ref[...] = jnp.zeros_like(z_ref)
    row = lax.broadcasted_iota(jnp.int32, (NB, NB), 0)
    col = lax.broadcasted_iota(jnp.int32, (NB, NB), 1)

    @pl.loop(0, blocks)
    def _(j):
        here = span(j * NB, NB, NB)
        aug[:, :NB] = rest[here, here]
        aug[:, NB:] = jnp.where(row == col, 1.0, 0.0)

        def between():
            for block in range(blocks):
                if (block, 0) in hooks:
                    pl.when(j == block)(hooks[block, 0])

        factor_block(aug, work, between)
        for block in range(blocks):
            @pl.when(j == block)
            def _():
                low, high = block * NB, (block + 1) * NB
                inverse = jnp.where(row >= col, work[:, NB:], 0.0)
                z_ref[low:high, low:high] = inverse
                if high < n:
                    column = dot_f32(rest[high:, low:high], inverse, NT)
                    lower[high:, low:high] = column
                    rest[high:, high:] = rest[high:, high:] - dot_f32(column, column, NT)
                if low:
                    z_ref[low:high, :low] = -dot_f32(
                        inverse, dot_f32(lower[low:high, :low], z_ref[:low, :low], NN), NN)
                hooks.get((block, 1), lambda: None)()


def whole_kernel(bases_ref, start_ref, modes_ref, *scratch):
    (slab, turned, a_ref, q_ref, e_sums, e_slots, part, part_low, work, first, second, lifted,
     z_ref, rest, lower, aug, factor_work) = scratch[:17]
    slots, sems, own_sem = scratch[17:-9], scratch[-9:-1], scratch[-1]
    pos = position()
    core = pos["core"]
    load = pltpu.make_async_copy(bases_ref, slab, own_sem.at[3])
    load.start()
    peers = batch_partners(pos, lax.axis_index("batch"), lax.axis_size("batch"))
    peers += [ring_peer(pos, "x", d) for d in (1, 2, 3)]
    peers += [ring_peer(pos, "z", d) for d in (1, 3)] + [sibling(pos)]

    def turn():
        turned[...] = start_ref[...].T

    greet(peers, turn)
    load.wait()
    energy = Energy(pos, e_sums, e_slots, Copies(*sems[6:]))
    exchange(pos, slab, turned, a_ref, q_ref, energy, Copies(*sems[:2]), own_sem)
    n, all_columns = lifted.shape
    chunks = all_columns // NB

    reduction = Reduction(
        pos, part.at[0], part_low.at[0], work.at[0], first, slots[:3 * COLOURS],
        Copies(*sems[2:4]), False,
    )
    early = reduction
    apply_gram(a_ref, lambda chunk: q_ref[chunk], lambda value, chunk: value, reduction)
    for number in range(6):
        if number < 4:
            energy.step(number)
        reduction.step(number)
    early.finish()
    scale = all_columns / energy.value()
    for chunk in range(chunks):
        here = slice(chunk * 256, (chunk + 1) * 256)
        first[core, here, :] = first[core, here, :] * scale + q_ref[chunk]
    over = Copies(*sems[2:4]).copy(
        18 * COLOURS, first.at[core], first.at[core], sibling(pos)
    )
    over.start()

    reduction = Reduction(
        pos, part.at[1], part_low.at[1], work.at[1], second, slots[3 * COLOURS:],
        Copies(*sems[4:6]), True,
    )

    def first_block(chunk):
        return first[core, chunk * 256:(chunk + 1) * 256, :]

    apply_gram(
        a_ref, first_block,
        lambda value, chunk: value * scale + first_block(chunk) * (1.0 / CHIPS), reduction,
    )

    def side(ref, half):
        return jnp.concatenate(
            [ref[half, chunk * 256:(chunk + 1) * 256, :] for chunk in range(chunks)], axis=1)

    over.wait()
    low = jnp.concatenate([side(first, half).astype(BF16) for half in range(2)], axis=0)
    rest[...] = dot_low(low, low, NT)
    sets = [range(3), range(3, 6)]
    inverse_factor(
        z_ref, rest, lower, aug, factor_work,
        {(stage + 1, part): functools.partial(reduction.step, stage, sets[part])
         for stage in range(3) for part in range(2)},
    )
    for stage in (3, 4, 5):
        reduction.step(stage)
    reduction.join()

    def times_factor(value_high, value_low, rows):
        z_stack = stack(z_ref[rows, :rows.stop])
        z_high = z_stack[:rows.stop - rows.start]
        return (fold(dot_low(z_stack, value_high[:rows.stop], NN))
                + dot_low(z_high, value_low[:rows.stop], NN))

    halves = [slice(0, n // 2), slice(n // 2, n)]
    blocks = 4
    width = all_columns // blocks
    rest[...] = jnp.zeros_like(rest)
    for block in range(blocks):
        value = jnp.concatenate(
            [jnp.concatenate(
                [second[half, chunk * 256:(chunk + 1) * 256, :]
                 for chunk in range(block * chunks // blocks, (block + 1) * chunks // blocks)],
                axis=1) for half in range(2)], axis=0)
        value_high, value_low = split(value)
        value = jnp.concatenate(
            [times_factor(value_high, value_low, rows) for rows in halves], axis=0)
        lifted[:, block * width:(block + 1) * width] = value
    both = stack(lifted[...])
    both = dot_low(both, both[:n], NT)
    rest[...] = both[:n] + both[n:] + both[n:].T
    inverse_factor(z_ref, rest, lower, aug, factor_work)

    height = modes_ref.shape[0]
    own_rows = span(core * height, height, 16)
    total = jnp.zeros(modes_ref.shape, F32)
    for block in range(blocks):
        here = slice(block * width, (block + 1) * width)
        value_high, value_low = split(lifted[:, here])
        q_low = jnp.concatenate(
            [times_factor(value_high, value_low, rows) for rows in halves], axis=0
        ).astype(BF16)
        total = total + dot_low(a_ref[own_rows, here], q_low, NT)
    modes_ref[...] = total.astype(BF16)
    reduction.finish()


def on_device(bases, start):
    count = lax.axis_size("batch")
    width, n = start.shape
    all_columns = width * count
    height = bases.shape[0] // count
    flat = all_columns * n // 2 // 128
    sems = lambda number: [pltpu.SemaphoreType.DMA((number,))] * 2
    slots = [
        pltpu.VMEM((3, size * u, 128), BF16 if size == 16 else F32)
        for u in UNITS for size in (16, 4, 1)
    ]
    return pl.pallas_call(
        whole_kernel,
        out_shape=jax.ShapeDtypeStruct((height, n), BF16),
        in_specs=[pl.BlockSpec(memory_space=pl.ANY), VMEM_SPEC],
        out_specs=VMEM_SPEC,
        scratch_shapes=[
            pltpu.VMEM(bases.shape, BF16),
            pltpu.VMEM((n, width), F32),
            pltpu.VMEM((2 * height, all_columns), BF16),
            pltpu.VMEM((flat // 256, 256, 128), F32),
            pltpu.VMEM((5, 8, 128), F32),
            pltpu.VMEM((4, 3, 8, 128), F32),
            pltpu.VMEM((2, flat, 128), F32),
            pltpu.VMEM((2, flat, 128), BF16),
            pltpu.VMEM((2, flat, 128), F32),
            pltpu.VMEM((2, flat, 128), F32),
            pltpu.VMEM((2, flat, 128), F32),
            pltpu.VMEM((n, all_columns), F32),
            pltpu.VMEM((n, n), F32),
            pltpu.VMEM((n, n), F32),
            pltpu.VMEM((n, n), F32),
            pltpu.VMEM((NB, 2 * NB), F32),
            pltpu.VMEM((NB, 2 * NB), F32),
            *slots, *slots,
            *sems(EXCHANGE_COPIES), *sems(REDUCE_COPIES), *sems(REDUCE_COPIES),
            *sems(ENERGY_COPIES),
            pltpu.SemaphoreType.DMA((4,)),
        ],
        compiler_params=pltpu.CompilerParams(
            collective_id=0, has_side_effects=True, vmem_limit_bytes=66_000_000
        ),
    )(bases, start)


def solution(mesh):
    in_specs = (P("rows", "batch"), P("batch", None))
    out_specs = P(("rows", "batch"), None)
    return jax.shard_map(
        on_device, mesh=mesh, in_specs=in_specs, out_specs=out_specs, check_vma=False
    )
```

```python
import functools

import jax
import jax.numpy as jnp
from jax import lax
from jax.experimental import pallas as pl
from jax.experimental.pallas import tpu as pltpu
from jax.sharding import PartitionSpec as P

NB = 128
GROUPS = 8
RING = 4
CHIPS = 64
ORDERS = (("x", "y", "z"), ("y", "z", "x"), ("z", "x", "y")) * 2
UNITS = (16, 8, 8, 8, 16, 8)
COLOURS = len(UNITS)
HIGHEST = lax.Precision.HIGHEST
VMEM_SPEC = pl.BlockSpec(memory_space=pltpu.VMEM)
F32, BF16 = jnp.float32, jnp.bfloat16
NN, NT, TN = ((1,), (0,)), ((1,), (1,)), ((0,), (0,))


def dot_f32(left, right, dims):
    return lax.dot_general(
        left, right, (dims, ((), ())), precision=HIGHEST, preferred_element_type=F32
    )


def dot_low(left, right, dims):
    return lax.dot_general(left, right, (dims, ((), ())), preferred_element_type=F32)


def split(value):
    high = value.astype(BF16)
    return high, (value - high.astype(F32)).astype(BF16)


def stack(value):
    return jnp.concatenate(split(value), axis=0)


def fold(value):
    half = value.shape[0] // 2
    return value[:half] + value[half:]


def span(start, size, unit):
    return pl.ds(pl.multiple_of(start, unit), size)


def position():
    rows, batch = lax.axis_index("rows"), lax.axis_index("batch")
    return {
        "x": rows // 2 % 4,
        "y": batch % 4,
        "z": batch // 4 * 2 + rows // 8,
        "core": rows % 2,
    }


def device_at(pos):
    return {
        "rows": pos["z"] % 2 * 8 + pos["x"] * 2 + pos["core"],
        "batch": pos["z"] // 2 * 4 + pos["y"],
    }


def ring_peer(pos, axis, distance):
    there = dict(pos)
    there[axis] = (pos[axis] + distance) % RING
    return there


def shifted(pos, shifts):
    there = dict(pos)
    for axis, distance in shifts.items():
        if distance:
            there[axis] = (pos[axis] + distance) % RING
    return there


def neighbours(pos):
    steps = range(RING)
    shifts = [{"x": a, "y": b, "z": c} for a in steps for b in steps for c in steps]
    return [
        shifted(pos, shift) for shift in shifts
        if 0 < sum(distance > 0 for distance in shift.values()) < 3
    ] + [sibling(pos)]


def sibling(pos):
    there = dict(pos)
    there["core"] = 1 - pos["core"]
    return there


def greet(peers, work):
    barrier = pltpu.get_barrier_semaphore()
    for peer in peers:
        pl.semaphore_signal(
            barrier, inc=1, device_id=device_at(peer), device_id_type=pl.DeviceIdType.MESH
        )
    work()
    pl.semaphore_wait(barrier, len(peers))


class Copies:
    def __init__(self, send_sem, recv_sem):
        self.send_sem, self.recv_sem = send_sem, recv_sem

    def copy(self, index, src, dst, peer):
        return pltpu.make_async_remote_copy(
            src_ref=src, dst_ref=dst,
            send_sem=self.send_sem.at[index], recv_sem=self.recv_sem.at[index],
            device_id=device_at(peer), device_id_type=pl.DeviceIdType.MESH,
        )


def batch_partners(pos, batch, count):
    partners = []
    for distance in range(1, count):
        other = (batch + distance) % count
        there = dict(pos)
        there["y"] = other % 4
        there["z"] = other // 4 * 2 + pos["z"] % 2
        partners.append(there)
    return partners


def exchange(pos, bases_ref, turned, a_ref, q_ref, energy, copies, own_sem):
    core, x = pos["core"], pos["x"]
    batch = lax.axis_index("batch")
    count = lax.axis_size("batch")
    height = bases_ref.shape[0] // count
    width = bases_ref.shape[1]
    quarter = 64
    partners = batch_partners(pos, batch, count)
    x_peers = [ring_peer(pos, "x", d) for d in (1, 2, 3)]
    made = []

    def start(src, dst, peer):
        copy = copies.copy(len(made), src, dst, peer)
        copy.start()
        made.append(copy)
        return copy

    own_rows = span(core * height, height, 16)
    mine = span(x * quarter, quarter, 8)
    turned_rows = span(core * 256 + x * quarter, quarter, 8)

    def columns(which):
        return span(which * width, width, 128)

    def block_rows(which):
        return span(which * height, height, 16)

    def piece(which, half):
        return q_ref.at[which * 2 + half, mine, :]

    own_start = []
    for half in range(2):
        own = pltpu.make_async_copy(
            turned.at[turned_rows, half * 128:(half + 1) * 128], piece(batch, half),
            own_sem.at[half],
        )
        own.start()
        own_start.append(own)
    start_in = [
        [start(turned.at[turned_rows, half * 128:(half + 1) * 128], piece(batch, half), there)
         for half in range(2)]
        for there in partners
    ]
    x_in = [
        start(turned.at[turned_rows, half * 128:(half + 1) * 128], piece(batch, half), there)
        for half in range(2) for there in x_peers
    ]
    block_in = [
        start(bases_ref.at[block_rows((batch + d) % count), :],
              a_ref.at[own_rows, columns(batch)], there)
        for d, there in enumerate(partners, 1)
    ]
    own_block = pltpu.make_async_copy(
        bases_ref.at[block_rows(batch), :], a_ref.at[own_rows, columns(batch)], own_sem.at[2]
    )
    own_block.start()
    aside = [
        start(bases_ref.at[block_rows(batch), :], a_ref.at[own_rows, columns(batch)],
              sibling(pos))
    ]

    def add_square(step, total):
        value = bases_ref[span(step * 64, 64, 64), :].astype(F32)
        value = value * value
        return total + jnp.sum(value.reshape(8, 8, 2 * 128), axis=0)

    total = lax.fori_loop(
        0, bases_ref.shape[0] // 64, add_square, jnp.zeros((8, 2 * 128), F32)
    )
    total = total[:, :128] + total[:, 128:]

    energy.begin(total)
    for distance, pair in enumerate(start_in, 1):
        for copy in pair:
            copy.wait_recv()
        other = (batch + count - distance) % count
        block = q_ref.at[span(other * 2, 2, 2), mine, :]
        x_in += [start(block, block, there) for there in x_peers]
    for copy in own_start:
        copy.wait()
    own_block.wait()
    for distance, copy in enumerate(block_in, 1):
        copy.wait_recv()
        other = (batch + count - distance) % count
        block = a_ref.at[own_rows, columns(other)]
        aside.append(start(block, block, sibling(pos)))
    for copy in x_in + aside:
        copy.wait_recv()
    for copy in made:
        copy.wait_send()


EXCHANGE_COPIES = 14 + 6 + 7 + 1 + 21 + 7


class Energy:
    def __init__(self, pos, sums, slots, copies):
        self.sums, self.slots, self.copies = sums, slots, copies
        self.rings = [[ring_peer(pos, axis, d) for d in (1, 2, 3)] for axis in "xyz"]
        self.rings.append([sibling(pos)])

    def copy(self, stage, slot):
        return self.copies.copy(
            3 * stage + slot, self.sums.at[stage], self.slots.at[stage, slot],
            self.rings[stage][slot],
        )

    def begin(self, total):
        self.sums[0] = total
        for slot in range(3):
            self.copy(0, slot).start()

    def step(self, stage):
        total = self.sums[stage]
        for slot in range(len(self.rings[stage])):
            self.copy(stage, slot).wait()
            total = total + self.slots[stage, slot]
        self.sums[stage + 1] = total
        if stage < 3:
            for slot in range(len(self.rings[stage + 1])):
                self.copy(stage + 1, slot).start()

    def value(self):
        return jnp.sum(self.sums[4], keepdims=True)


ENERGY_COPIES = 10


PLANE = [(a, b) for a in range(RING) for b in range(RING) if a or b]


class Reduction:
    def __init__(self, pos, part, part_low, work, out, slots, copies, forward):
        self.pos, self.part, self.work, self.out = pos, part, work, out
        self.part_low, self.forward = part_low, forward
        self.slots, self.copies = slots, copies
        self.base = [CHIPS * sum(UNITS[:k]) for k in range(COLOURS)]

    def first(self, k):
        return self.pos[ORDERS[k][0]]

    def origin(self, k):
        return self.base[k] + self.first(k) * 16 * UNITS[k]

    def place(self, k, a, b):
        _, one, two = ORDERS[k]
        index = (self.pos[one] + a) % RING * RING + (self.pos[two] + b) % RING
        return self.origin(k) + index * UNITS[k]

    def peer(self, k, a, b):
        return shifted(self.pos, {ORDERS[k][1]: a, ORDERS[k][2]: b})

    def ring_peer(self, k, d):
        return ring_peer(self.pos, ORDERS[k][0], d)

    def block(self, start, size):
        return self.out.at[self.pos["core"], span(start, size, 8), :]

    def ring_sum(self, k, d):
        size = 16 * UNITS[k]
        target = (self.first(k) + d) % RING
        return self.copies.copy(
            40 * k + d - 1, self.part_low.at[span(self.base[k] + target * size, size, 16), :],
            self.slots[2 * k].at[d - 1], self.ring_peer(k, d),
        )

    def plane_sum(self, k, slot):
        a, b = PLANE[slot]
        return self.copies.copy(
            40 * k + 3 + slot, self.work.at[span(self.place(k, a, b), UNITS[k], 8), :],
            self.slots[2 * k + 1].at[slot], self.peer(k, a, b),
        )

    def plane_gather(self, k, slot):
        block = self.block(self.place(k, 0, 0), UNITS[k])
        return self.copies.copy(40 * k + 18 + slot, block, block, self.peer(k, *PLANE[slot]))

    def ring_gather(self, k, d):
        block = self.block(self.origin(k), 16 * UNITS[k])
        return self.copies.copy(40 * k + 33 + d - 1, block, block, self.ring_peer(k, d))

    def aside_copy(self, k, d):
        size = 16 * UNITS[k]
        sender = (self.first(k) + RING - d) % RING
        block = self.block(self.base[k] + sender * size, size)
        return self.copies.copy(40 * k + 36 + d, block, block, sibling(self.pos))

    def start(self, k):
        for d in (1, 2, 3):
            self.ring_sum(k, d).start()

    def step(self, number, colours=range(COLOURS)):
        for k in colours:
            if number == 0:
                for d in (1, 2, 3):
                    self.ring_sum(k, d).wait_recv()
                here = span(self.origin(k), 16 * UNITS[k], 8)
                value = self.part[here, :]
                for d in range(3):
                    value = value + self.slots[2 * k][d].astype(F32)
                self.work[here, :] = value
                for slot in range(len(PLANE)):
                    self.plane_sum(k, slot).start()
            elif number == 1:
                here = span(self.place(k, 0, 0), UNITS[k], 8)
                value = self.work[here, :]
                for slot in range(len(PLANE)):
                    self.plane_sum(k, slot).wait_recv()
                    value = value + self.slots[2 * k + 1][slot]
                self.out[self.pos["core"], here, :] = value
                for slot in range(len(PLANE)):
                    self.plane_gather(k, slot).start()
            elif number == 2:
                for slot in range(len(PLANE)):
                    self.plane_gather(k, slot).wait_recv()
                for d in (1, 2, 3):
                    self.ring_gather(k, d).start()
                if self.forward:
                    self.aside_copy(k, 0).start()
            else:
                for d in (1, 2, 3):
                    self.ring_gather(k, d).wait_recv()
                    if self.forward:
                        self.aside_copy(k, d).start()

    def join(self):
        for k in range(COLOURS):
            for d in range(4):
                self.aside_copy(k, d).wait_recv()

    def finish(self):
        for k in range(COLOURS):
            if self.forward:
                for d in range(4):
                    self.aside_copy(k, d).wait_send()
            for d in (1, 2, 3):
                self.ring_sum(k, d).wait_send()
                self.ring_gather(k, d).wait_send()
            for slot in range(len(PLANE)):
                self.plane_sum(k, slot).wait_send()
                self.plane_gather(k, slot).wait_send()


REDUCE_COPIES = 40 * COLOURS


def apply_gram(a_ref, q_block, combine, reduction):
    chunks = a_ref.shape[1] // 128
    q = jnp.concatenate([q_block(chunk) for chunk in range(chunks)], axis=1)
    inner = stack(fold(dot_low(stack(q), a_ref[...], NT)))
    ready = 0
    for block in range(chunks // 2):
        value = fold(dot_low(inner, a_ref[:, block * 256:(block + 1) * 256], NN))
        for half in range(2):
            chunk = 2 * block + half
            share = combine(value[:, half * 128:(half + 1) * 128], chunk)
            here = slice(chunk * 256, (chunk + 1) * 256)
            reduction.part[here, :] = share
            reduction.part_low[here, :] = share.astype(BF16)
        while ready < COLOURS and CHIPS * sum(UNITS[:ready + 1]) <= (block + 1) * 512:
            reduction.start(ready)
            ready += 1


def factor_block(aug, work, between=lambda: None):
    row = lax.broadcasted_iota(jnp.int32, (8, NB), 0)
    height = 8 * GROUPS
    for panel in range(NB // height):
        low = height * panel
        left = [aug[low + 8 * g:low + 8 * g + 8, :NB] for g in range(GROUPS)]
        right = [aug[low + 8 * g:low + 8 * g + 8, NB:] for g in range(GROUPS)]
        for s in range(GROUPS):
            rest = range(s, GROUPS)
            lane = low + 8 * s
            cols = {
                (g, k): jnp.broadcast_to(left[g][:, lane + k:lane + k + 1], (8, NB))
                for g in rest for k in range(8)
            }
            pivots = jnp.zeros((8, NB), F32)
            for k in range(8):
                pivot = jnp.broadcast_to(cols[s, k][k:k + 1, :], (8, NB))
                inverse = 1.0 / pivot
                pivots = jnp.where(row == k, pivot, pivots)
                mult = {g: cols[g, k] * inverse for g in rest}
                mult[s] = jnp.where(row > k, mult[s], 0.0)
                for j in range(k + 1, 8):
                    value = jnp.broadcast_to(cols[s, j][k:k + 1, :], (8, NB))
                    for g in rest:
                        cols[g, j] = cols[g, j] - mult[g] * value
                left_row = jnp.broadcast_to(left[s][k:k + 1, :], (8, NB))
                right_row = jnp.broadcast_to(right[s][k:k + 1, :], (8, NB))
                for g in rest:
                    left[g] = left[g] - mult[g] * left_row
                    right[g] = right[g] - mult[g] * right_row
            scale = lax.rsqrt(pivots)
            work[lane:lane + 8, :NB] = left[s] * scale
            work[lane:lane + 8, NB:] = right[s] * scale
        if low + height < NB:
            rows = work[low:low + height, :]
            aug[low + height:, :] = (
                aug[low + height:, :] - dot_f32(rows[:, :NB], rows, TN)[low + height:, :])
            between()


def inverse_factor(z_ref, rest, lower, aug, work, hooks={}):
    n = rest.shape[0]
    blocks = n // NB
    z_ref[...] = jnp.zeros_like(z_ref)
    row = lax.broadcasted_iota(jnp.int32, (NB, NB), 0)
    col = lax.broadcasted_iota(jnp.int32, (NB, NB), 1)

    @pl.loop(0, blocks)
    def _(j):
        here = span(j * NB, NB, NB)
        aug[:, :NB] = rest[here, here]
        aug[:, NB:] = jnp.where(row == col, 1.0, 0.0)

        def between():
            for block in range(blocks):
                if (block, 0) in hooks:
                    pl.when(j == block)(hooks[block, 0])

        factor_block(aug, work, between)
        for block in range(blocks):
            @pl.when(j == block)
            def _():
                low, high = block * NB, (block + 1) * NB
                inverse = jnp.where(row >= col, work[:, NB:], 0.0)
                z_ref[low:high, low:high] = inverse
                if high < n:
                    column = dot_f32(rest[high:, low:high], inverse, NT)
                    lower[high:, low:high] = column
                    rest[high:, high:] = rest[high:, high:] - dot_f32(column, column, NT)
                if low:
                    z_ref[low:high, :low] = -dot_f32(
                        inverse, dot_f32(lower[low:high, :low], z_ref[:low, :low], NN), NN)
                hooks.get((block, 1), lambda: None)()


def whole_kernel(bases_ref, start_ref, modes_ref, *scratch):
    (slab, turned, a_ref, q_ref, e_sums, e_slots, part, part_low, work, first, second, lifted,
     z_ref, rest, lower, aug, factor_work) = scratch[:17]
    slots, sems, own_sem = scratch[17:-9], scratch[-9:-1], scratch[-1]
    pos = position()
    core = pos["core"]
    load = pltpu.make_async_copy(bases_ref, slab, own_sem.at[3])
    load.start()
    def turn():
        turned[...] = start_ref[...].T

    greet(neighbours(pos), turn)
    load.wait()
    energy = Energy(pos, e_sums, e_slots, Copies(*sems[6:]))
    exchange(pos, slab, turned, a_ref, q_ref, energy, Copies(*sems[:2]), own_sem)
    n, all_columns = lifted.shape
    chunks = all_columns // NB

    reduction = Reduction(
        pos, part.at[0], part_low.at[0], work.at[0], first, slots[:2 * COLOURS],
        Copies(*sems[2:4]), False,
    )
    early = reduction
    apply_gram(a_ref, lambda chunk: q_ref[chunk], lambda value, chunk: value, reduction)
    for number in range(4):
        energy.step(number)
        reduction.step(number)
    early.finish()
    scale = all_columns / energy.value()
    for chunk in range(chunks):
        here = slice(chunk * 256, (chunk + 1) * 256)
        first[core, here, :] = first[core, here, :] * scale + q_ref[chunk]
    over = Copies(*sems[2:4]).copy(
        36, first.at[core], first.at[core], sibling(pos)
    )
    over.start()

    reduction = Reduction(
        pos, part.at[1], part_low.at[1], work.at[1], second, slots[2 * COLOURS:],
        Copies(*sems[4:6]), True,
    )

    def first_block(chunk):
        return first[core, chunk * 256:(chunk + 1) * 256, :]

    apply_gram(
        a_ref, first_block,
        lambda value, chunk: value * scale + first_block(chunk) * (1.0 / CHIPS), reduction,
    )

    def side(ref, half):
        return jnp.concatenate(
            [ref[half, chunk * 256:(chunk + 1) * 256, :] for chunk in range(chunks)], axis=1)

    over.wait()
    low = jnp.concatenate([side(first, half).astype(BF16) for half in range(2)], axis=0)
    rest[...] = dot_low(low, low, NT)
    places = [(0, 0), (0, 1), (1, 1), (2, 0), (2, 1), (3, 0)]
    parts = [(number, range(3 * part, 3 * part + 3)) for number in range(3) for part in range(2)]
    inverse_factor(
        z_ref, rest, lower, aug, factor_work,
        {place: functools.partial(reduction.step, *part) for place, part in zip(places, parts)},
    )
    reduction.step(3)
    reduction.join()

    def times_factor(value_high, value_low, rows):
        z_stack = stack(z_ref[rows, :rows.stop])
        z_high = z_stack[:rows.stop - rows.start]
        return (fold(dot_low(z_stack, value_high[:rows.stop], NN))
                + dot_low(z_high, value_low[:rows.stop], NN))

    halves = [slice(0, n // 2), slice(n // 2, n)]
    blocks = 4
    width = all_columns // blocks
    rest[...] = jnp.zeros_like(rest)
    for block in range(blocks):
        value = jnp.concatenate(
            [jnp.concatenate(
                [second[half, chunk * 256:(chunk + 1) * 256, :]
                 for chunk in range(block * chunks // blocks, (block + 1) * chunks // blocks)],
                axis=1) for half in range(2)], axis=0)
        value_high, value_low = split(value)
        value = jnp.concatenate(
            [times_factor(value_high, value_low, rows) for rows in halves], axis=0)
        lifted[:, block * width:(block + 1) * width] = value
    both = stack(lifted[...])
    both = dot_low(both, both[:n], NT)
    rest[...] = both[:n] + both[n:] + both[n:].T
    inverse_factor(z_ref, rest, lower, aug, factor_work)

    height = modes_ref.shape[0]
    own_rows = span(core * height, height, 16)
    total = jnp.zeros(modes_ref.shape, F32)
    for block in range(blocks):
        here = slice(block * width, (block + 1) * width)
        value_high, value_low = split(lifted[:, here])
        q_low = jnp.concatenate(
            [times_factor(value_high, value_low, rows) for rows in halves], axis=0
        ).astype(BF16)
        total = total + dot_low(a_ref[own_rows, here], q_low, NT)
    modes_ref[...] = total.astype(BF16)
    reduction.finish()


def on_device(bases, start):
    count = lax.axis_size("batch")
    width, n = start.shape
    all_columns = width * count
    height = bases.shape[0] // count
    flat = all_columns * n // 2 // 128
    sems = lambda number: [pltpu.SemaphoreType.DMA((number,))] * 2
    slots = []
    for unit in UNITS:
        slots.append(pltpu.VMEM((3, 16 * unit, 128), BF16))
        slots.append(pltpu.VMEM((len(PLANE), unit, 128), F32))
    return pl.pallas_call(
        whole_kernel,
        out_shape=jax.ShapeDtypeStruct((height, n), BF16),
        in_specs=[pl.BlockSpec(memory_space=pl.ANY), VMEM_SPEC],
        out_specs=VMEM_SPEC,
        scratch_shapes=[
            pltpu.VMEM(bases.shape, BF16),
            pltpu.VMEM((n, width), F32),
            pltpu.VMEM((2 * height, all_columns), BF16),
            pltpu.VMEM((flat // 256, 256, 128), F32),
            pltpu.VMEM((5, 8, 128), F32),
            pltpu.VMEM((4, 3, 8, 128), F32),
            pltpu.VMEM((2, flat, 128), F32),
            pltpu.VMEM((2, flat, 128), BF16),
            pltpu.VMEM((2, flat, 128), F32),
            pltpu.VMEM((2, flat, 128), F32),
            pltpu.VMEM((2, flat, 128), F32),
            pltpu.VMEM((n, all_columns), F32),
            pltpu.VMEM((n, n), F32),
            pltpu.VMEM((n, n), F32),
            pltpu.VMEM((n, n), F32),
            pltpu.VMEM((NB, 2 * NB), F32),
            pltpu.VMEM((NB, 2 * NB), F32),
            *slots, *slots,
            *sems(EXCHANGE_COPIES), *sems(REDUCE_COPIES), *sems(REDUCE_COPIES),
            *sems(ENERGY_COPIES),
            pltpu.SemaphoreType.DMA((4,)),
        ],
        compiler_params=pltpu.CompilerParams(
            collective_id=0, has_side_effects=True, vmem_limit_bytes=66_000_000
        ),
    )(bases, start)


def solution(mesh):
    in_specs = (P("rows", "batch"), P("batch", None))
    out_specs = P(("rows", "batch"), None)
    return jax.shard_map(
        on_device, mesh=mesh, in_specs=in_specs, out_specs=out_specs, check_vma=False
    )
```

```python
import functools

import jax
import jax.numpy as jnp
from jax import lax
from jax.experimental import pallas as pl
from jax.experimental.pallas import tpu as pltpu
from jax.sharding import PartitionSpec as P

NB = 128
GROUPS = 8
RING = 4
CHIPS = 64
ORDERS = (("x", "y", "z"), ("y", "z", "x"), ("z", "x", "y")) * 2
UNITS = (16, 8, 8, 8, 16, 8)
COLOURS = len(UNITS)
HIGHEST = lax.Precision.HIGHEST
VMEM_SPEC = pl.BlockSpec(memory_space=pltpu.VMEM)
F32, BF16 = jnp.float32, jnp.bfloat16
NN, NT, TN = ((1,), (0,)), ((1,), (1,)), ((0,), (0,))


def dot_f32(left, right, dims):
    return lax.dot_general(
        left, right, (dims, ((), ())), precision=HIGHEST, preferred_element_type=F32
    )


def dot_low(left, right, dims):
    return lax.dot_general(left, right, (dims, ((), ())), preferred_element_type=F32)


def split(value):
    high = value.astype(BF16)
    return high, (value - high.astype(F32)).astype(BF16)


def stack(value):
    return jnp.concatenate(split(value), axis=0)


def fold(value):
    half = value.shape[0] // 2
    return value[:half] + value[half:]


def span(start, size, unit):
    return pl.ds(pl.multiple_of(start, unit), size)


def position():
    rows, batch = lax.axis_index("rows"), lax.axis_index("batch")
    return {
        "x": rows // 2 % 4,
        "y": batch % 4,
        "z": batch // 4 * 2 + rows // 8,
        "core": rows % 2,
    }


def device_at(pos):
    return {
        "rows": pos["z"] % 2 * 8 + pos["x"] * 2 + pos["core"],
        "batch": pos["z"] // 2 * 4 + pos["y"],
    }


def ring_peer(pos, axis, distance):
    there = dict(pos)
    there[axis] = (pos[axis] + distance) % RING
    return there


def shifted(pos, shifts):
    there = dict(pos)
    for axis, distance in shifts.items():
        if distance:
            there[axis] = (pos[axis] + distance) % RING
    return there


def axis_peers(pos):
    return [ring_peer(pos, axis, d) for axis in "xyz" for d in (1, 2, 3)]


def sibling(pos):
    there = dict(pos)
    there["core"] = 1 - pos["core"]
    return there


def greet(peers, work):
    barrier = pltpu.get_barrier_semaphore()
    for peer in peers:
        pl.semaphore_signal(
            barrier, inc=1, device_id=device_at(peer), device_id_type=pl.DeviceIdType.MESH
        )
    work()
    pl.semaphore_wait(barrier, len(peers))


class Copies:
    def __init__(self, send_sem, recv_sem):
        self.send_sem, self.recv_sem = send_sem, recv_sem

    def copy(self, index, src, dst, peer):
        return pltpu.make_async_remote_copy(
            src_ref=src, dst_ref=dst,
            send_sem=self.send_sem.at[index], recv_sem=self.recv_sem.at[index],
            device_id=device_at(peer), device_id_type=pl.DeviceIdType.MESH,
        )


def batch_partners(pos, batch, count):
    partners = []
    for distance in range(1, count):
        other = (batch + distance) % count
        there = dict(pos)
        there["y"] = other % 4
        there["z"] = other // 4 * 2 + pos["z"] % 2
        partners.append(there)
    return partners


def exchange(pos, bases_ref, turned, a_ref, q_ref, energy, copies, own_sem):
    core, x = pos["core"], pos["x"]
    batch = lax.axis_index("batch")
    count = lax.axis_size("batch")
    height = bases_ref.shape[0] // count
    width = bases_ref.shape[1]
    quarter = 64
    partners = batch_partners(pos, batch, count)
    x_peers = [ring_peer(pos, "x", d) for d in (1, 2, 3)]
    made = []

    def start(src, dst, peer):
        copy = copies.copy(len(made), src, dst, peer)
        copy.start()
        made.append(copy)
        return copy

    own_rows = span(core * height, height, 16)
    mine = span(x * quarter, quarter, 8)
    turned_rows = span(core * 256 + x * quarter, quarter, 8)

    def columns(which):
        return span(which * width, width, 128)

    def block_rows(which):
        return span(which * height, height, 16)

    def piece(which, half):
        return q_ref.at[which * 2 + half, mine, :]

    own_start = []
    for half in range(2):
        own = pltpu.make_async_copy(
            turned.at[turned_rows, half * 128:(half + 1) * 128], piece(batch, half),
            own_sem.at[half],
        )
        own.start()
        own_start.append(own)
    start_in = [
        [start(turned.at[turned_rows, half * 128:(half + 1) * 128], piece(batch, half), there)
         for half in range(2)]
        for there in partners
    ]
    x_in = [
        start(turned.at[turned_rows, half * 128:(half + 1) * 128], piece(batch, half), there)
        for half in range(2) for there in x_peers
    ]
    block_in = [
        start(bases_ref.at[block_rows((batch + d) % count), :],
              a_ref.at[own_rows, columns(batch)], there)
        for d, there in enumerate(partners, 1)
    ]
    own_block = pltpu.make_async_copy(
        bases_ref.at[block_rows(batch), :], a_ref.at[own_rows, columns(batch)], own_sem.at[2]
    )
    own_block.start()
    aside = [
        start(bases_ref.at[block_rows(batch), :], a_ref.at[own_rows, columns(batch)],
              sibling(pos))
    ]

    def add_square(step, total):
        value = bases_ref[span(step * 64, 64, 64), :].astype(F32)
        value = value * value
        return total + jnp.sum(value.reshape(8, 8, 2 * 128), axis=0)

    total = lax.fori_loop(
        0, bases_ref.shape[0] // 64, add_square, jnp.zeros((8, 2 * 128), F32)
    )
    total = total[:, :128] + total[:, 128:]

    energy.begin(total)
    for distance, pair in enumerate(start_in, 1):
        for copy in pair:
            copy.wait_recv()
        other = (batch + count - distance) % count
        block = q_ref.at[span(other * 2, 2, 2), mine, :]
        x_in += [start(block, block, there) for there in x_peers]
    for copy in own_start:
        copy.wait()
    own_block.wait()
    for distance, copy in enumerate(block_in, 1):
        copy.wait_recv()
        other = (batch + count - distance) % count
        block = a_ref.at[own_rows, columns(other)]
        aside.append(start(block, block, sibling(pos)))
    for copy in x_in + aside:
        copy.wait_recv()
    for copy in made:
        copy.wait_send()


EXCHANGE_COPIES = 14 + 6 + 7 + 1 + 21 + 7


class Energy:
    def __init__(self, pos, sums, slots, copies):
        self.sums, self.slots, self.copies = sums, slots, copies
        self.rings = [[ring_peer(pos, axis, d) for d in (1, 2, 3)] for axis in "xyz"]
        self.rings.append([sibling(pos)])

    def copy(self, stage, slot):
        return self.copies.copy(
            3 * stage + slot, self.sums.at[stage], self.slots.at[stage, slot],
            self.rings[stage][slot],
        )

    def begin(self, total):
        self.sums[0] = total
        for slot in range(3):
            self.copy(0, slot).start()

    def step(self, stage):
        total = self.sums[stage]
        for slot in range(len(self.rings[stage])):
            self.copy(stage, slot).wait()
            total = total + self.slots[stage, slot]
        self.sums[stage + 1] = total
        if stage < 3:
            for slot in range(len(self.rings[stage + 1])):
                self.copy(stage + 1, slot).start()

    def value(self):
        return jnp.sum(self.sums[4], keepdims=True)


ENERGY_COPIES = 10


PLANE = [(a, b) for a in range(RING) for b in range(RING) if a or b]


class Reduction:
    def __init__(self, pos, part, part_low, work, out, slots, copies, forward):
        self.pos, self.part, self.work, self.out = pos, part, work, out
        self.part_low, self.forward = part_low, forward
        self.slots, self.copies = slots, copies
        self.base = [CHIPS * sum(UNITS[:k]) for k in range(COLOURS)]

    def first(self, k):
        return self.pos[ORDERS[k][0]]

    def origin(self, k):
        return self.base[k] + self.first(k) * 16 * UNITS[k]

    def place(self, k, a, b):
        _, one, two = ORDERS[k]
        index = (self.pos[one] + a) % RING * RING + (self.pos[two] + b) % RING
        return self.origin(k) + index * UNITS[k]

    def peer(self, k, a, b):
        return shifted(self.pos, {ORDERS[k][1]: a, ORDERS[k][2]: b})

    def ring_peer(self, k, d):
        return ring_peer(self.pos, ORDERS[k][0], d)

    def block(self, start, size):
        return self.out.at[self.pos["core"], span(start, size, 8), :]

    def ring_sum(self, k, d):
        size = 16 * UNITS[k]
        target = (self.first(k) + d) % RING
        return self.copies.copy(
            40 * k + d - 1, self.part_low.at[span(self.base[k] + target * size, size, 16), :],
            self.slots[2 * k].at[d - 1], self.ring_peer(k, d),
        )

    def plane_sum(self, k, slot):
        a, b = PLANE[slot]
        return self.copies.copy(
            40 * k + 3 + slot, self.work.at[span(self.place(k, a, b), UNITS[k], 8), :],
            self.slots[2 * k + 1].at[slot], self.peer(k, a, b),
        )

    def plane_gather(self, k, slot):
        block = self.block(self.place(k, 0, 0), UNITS[k])
        return self.copies.copy(40 * k + 18 + slot, block, block, self.peer(k, *PLANE[slot]))

    def ring_gather(self, k, d):
        block = self.block(self.origin(k), 16 * UNITS[k])
        return self.copies.copy(40 * k + 33 + d - 1, block, block, self.ring_peer(k, d))

    def aside_copy(self, k, d):
        size = 16 * UNITS[k]
        sender = (self.first(k) + RING - d) % RING
        block = self.block(self.base[k] + sender * size, size)
        return self.copies.copy(40 * k + 36 + d, block, block, sibling(self.pos))

    def start(self, k):
        for d in (1, 2, 3):
            self.ring_sum(k, d).start()

    def step(self, number, colours=range(COLOURS)):
        for k in colours:
            if number == 0:
                for d in (1, 2, 3):
                    self.ring_sum(k, d).wait_recv()
                here = span(self.origin(k), 16 * UNITS[k], 8)
                value = self.part[here, :]
                for d in range(3):
                    value = value + self.slots[2 * k][d].astype(F32)
                self.work[here, :] = value
                for slot in range(len(PLANE)):
                    self.plane_sum(k, slot).start()
            elif number == 1:
                here = span(self.place(k, 0, 0), UNITS[k], 8)
                value = self.work[here, :]
                for slot in range(len(PLANE)):
                    self.plane_sum(k, slot).wait_recv()
                    value = value + self.slots[2 * k + 1][slot]
                self.out[self.pos["core"], here, :] = value
                for slot in range(len(PLANE)):
                    self.plane_gather(k, slot).start()
            elif number == 2:
                for slot in range(len(PLANE)):
                    self.plane_gather(k, slot).wait_recv()
                for d in (1, 2, 3):
                    self.ring_gather(k, d).start()
                if self.forward:
                    self.aside_copy(k, 0).start()
            else:
                for d in (1, 2, 3):
                    self.ring_gather(k, d).wait_recv()
                    if self.forward:
                        self.aside_copy(k, d).start()

    def join(self):
        for k in range(COLOURS):
            for d in range(4):
                self.aside_copy(k, d).wait_recv()

    def finish(self):
        for k in range(COLOURS):
            if self.forward:
                for d in range(4):
                    self.aside_copy(k, d).wait_send()
            for d in (1, 2, 3):
                self.ring_sum(k, d).wait_send()
                self.ring_gather(k, d).wait_send()
            for slot in range(len(PLANE)):
                self.plane_sum(k, slot).wait_send()
                self.plane_gather(k, slot).wait_send()


REDUCE_COPIES = 40 * COLOURS


def apply_gram(a_ref, q_block, combine, reduction):
    chunks = a_ref.shape[1] // 128
    q = jnp.concatenate([q_block(chunk) for chunk in range(chunks)], axis=1)
    inner = stack(fold(dot_low(stack(q), a_ref[...], NT)))
    ready = 0
    for block in range(chunks // 2):
        value = fold(dot_low(inner, a_ref[:, block * 256:(block + 1) * 256], NN))
        for half in range(2):
            chunk = 2 * block + half
            share = combine(value[:, half * 128:(half + 1) * 128], chunk)
            here = slice(chunk * 256, (chunk + 1) * 256)
            reduction.part[here, :] = share
            reduction.part_low[here, :] = share.astype(BF16)
        while ready < COLOURS and CHIPS * sum(UNITS[:ready + 1]) <= (block + 1) * 512:
            reduction.start(ready)
            ready += 1


def factor_block(aug, work, between=lambda: None):
    row = lax.broadcasted_iota(jnp.int32, (8, NB), 0)
    height = 8 * GROUPS
    for panel in range(NB // height):
        low = height * panel
        left = [aug[low + 8 * g:low + 8 * g + 8, :NB] for g in range(GROUPS)]
        right = [aug[low + 8 * g:low + 8 * g + 8, NB:] for g in range(GROUPS)]
        for s in range(GROUPS):
            rest = range(s, GROUPS)
            lane = low + 8 * s
            cols = {
                (g, k): jnp.broadcast_to(left[g][:, lane + k:lane + k + 1], (8, NB))
                for g in rest for k in range(8)
            }
            pivots = jnp.zeros((8, NB), F32)
            for k in range(8):
                pivot = jnp.broadcast_to(cols[s, k][k:k + 1, :], (8, NB))
                inverse = 1.0 / pivot
                pivots = jnp.where(row == k, pivot, pivots)
                mult = {g: cols[g, k] * inverse for g in rest}
                mult[s] = jnp.where(row > k, mult[s], 0.0)
                for j in range(k + 1, 8):
                    value = jnp.broadcast_to(cols[s, j][k:k + 1, :], (8, NB))
                    for g in rest:
                        cols[g, j] = cols[g, j] - mult[g] * value
                left_row = jnp.broadcast_to(left[s][k:k + 1, :], (8, NB))
                right_row = jnp.broadcast_to(right[s][k:k + 1, :], (8, NB))
                for g in rest:
                    left[g] = left[g] - mult[g] * left_row
                    right[g] = right[g] - mult[g] * right_row
            scale = lax.rsqrt(pivots)
            work[lane:lane + 8, :NB] = left[s] * scale
            work[lane:lane + 8, NB:] = right[s] * scale
        if low + height < NB:
            rows = work[low:low + height, :]
            aug[low + height:, :] = (
                aug[low + height:, :] - dot_f32(rows[:, :NB], rows, TN)[low + height:, :])
            between()


def inverse_factor(z_ref, rest, lower, aug, work, hooks={}):
    n = rest.shape[0]
    blocks = n // NB
    z_ref[...] = jnp.zeros_like(z_ref)
    row = lax.broadcasted_iota(jnp.int32, (NB, NB), 0)
    col = lax.broadcasted_iota(jnp.int32, (NB, NB), 1)

    @pl.loop(0, blocks)
    def _(j):
        here = span(j * NB, NB, NB)
        aug[:, :NB] = rest[here, here]
        aug[:, NB:] = jnp.where(row == col, 1.0, 0.0)

        def between():
            for block in range(blocks):
                if (block, 0) in hooks:
                    pl.when(j == block)(hooks[block, 0])

        factor_block(aug, work, between)
        for block in range(blocks):
            @pl.when(j == block)
            def _():
                low, high = block * NB, (block + 1) * NB
                inverse = jnp.where(row >= col, work[:, NB:], 0.0)
                z_ref[low:high, low:high] = inverse
                if high < n:
                    column = dot_f32(rest[high:, low:high], inverse, NT)
                    lower[high:, low:high] = column
                    rest[high:, high:] = rest[high:, high:] - dot_f32(column, column, NT)
                if low:
                    z_ref[low:high, :low] = -dot_f32(
                        inverse, dot_f32(lower[low:high, :low], z_ref[:low, :low], NN), NN)
                hooks.get((block, 1), lambda: None)()


def whole_kernel(bases_ref, start_ref, modes_ref, *scratch):
    (slab, turned, a_ref, q_ref, e_sums, e_slots, part, part_low, work, first, second, lifted,
     z_ref, rest, lower, aug, factor_work) = scratch[:17]
    slots, sems, own_sem, entered = scratch[17:-10], scratch[-10:-2], scratch[-2], scratch[-1]
    pos = position()
    core = pos["core"]
    load = pltpu.make_async_copy(bases_ref, slab, own_sem.at[3])
    load.start()
    def turn():
        turned[...] = start_ref[...].T

    peers = batch_partners(pos, lax.axis_index("batch"), lax.axis_size("batch"))
    peers += [ring_peer(pos, "x", d) for d in (1, 2, 3)]
    peers += [ring_peer(pos, "z", d) for d in (1, 3)] + [sibling(pos)]
    greet(peers, turn)
    for peer in axis_peers(pos):
        pl.semaphore_signal(
            entered, inc=1, device_id=device_at(peer), device_id_type=pl.DeviceIdType.MESH
        )
    load.wait()
    energy = Energy(pos, e_sums, e_slots, Copies(*sems[6:]))
    exchange(pos, slab, turned, a_ref, q_ref, energy, Copies(*sems[:2]), own_sem)
    n, all_columns = lifted.shape
    chunks = all_columns // NB

    reduction = Reduction(
        pos, part.at[0], part_low.at[0], work.at[0], first, slots[:2 * COLOURS],
        Copies(*sems[2:4]), False,
    )
    early = reduction
    apply_gram(a_ref, lambda chunk: q_ref[chunk], lambda value, chunk: value, reduction)
    pl.semaphore_wait(entered, 9)
    for number in range(4):
        energy.step(number)
        reduction.step(number)
    early.finish()
    scale = all_columns / energy.value()
    for chunk in range(chunks):
        here = slice(chunk * 256, (chunk + 1) * 256)
        first[core, here, :] = first[core, here, :] * scale + q_ref[chunk]
    over = Copies(*sems[2:4]).copy(
        36, first.at[core], first.at[core], sibling(pos)
    )
    over.start()

    reduction = Reduction(
        pos, part.at[1], part_low.at[1], work.at[1], second, slots[2 * COLOURS:],
        Copies(*sems[4:6]), True,
    )

    def first_block(chunk):
        return first[core, chunk * 256:(chunk + 1) * 256, :]

    apply_gram(
        a_ref, first_block,
        lambda value, chunk: value * scale + first_block(chunk) * (1.0 / CHIPS), reduction,
    )

    def side(ref, half):
        return jnp.concatenate(
            [ref[half, chunk * 256:(chunk + 1) * 256, :] for chunk in range(chunks)], axis=1)

    over.wait()
    low = jnp.concatenate([side(first, half).astype(BF16) for half in range(2)], axis=0)
    rest[...] = dot_low(low, low, NT)
    places = [(0, 0), (0, 1), (1, 0), (1, 1), (2, 0), (2, 1), (3, 0), (3, 1)]
    parts = [(number, range(3 * part, 3 * part + 3)) for number in range(4) for part in range(2)]
    inverse_factor(
        z_ref, rest, lower, aug, factor_work,
        {place: functools.partial(reduction.step, *part) for place, part in zip(places, parts)},
    )
    reduction.join()

    def times_factor(value_high, value_low, rows):
        z_stack = stack(z_ref[rows, :rows.stop])
        z_high = z_stack[:rows.stop - rows.start]
        return (fold(dot_low(z_stack, value_high[:rows.stop], NN))
                + dot_low(z_high, value_low[:rows.stop], NN))

    halves = [slice(0, n // 2), slice(n // 2, n)]
    blocks = 4
    width = all_columns // blocks
    rest[...] = jnp.zeros_like(rest)
    for block in range(blocks):
        value = jnp.concatenate(
            [jnp.concatenate(
                [second[half, chunk * 256:(chunk + 1) * 256, :]
                 for chunk in range(block * chunks // blocks, (block + 1) * chunks // blocks)],
                axis=1) for half in range(2)], axis=0)
        value_high, value_low = split(value)
        value = jnp.concatenate(
            [times_factor(value_high, value_low, rows) for rows in halves], axis=0)
        lifted[:, block * width:(block + 1) * width] = value
    both = stack(lifted[...])
    both = dot_low(both, both[:n], NT)
    rest[...] = both[:n] + both[n:] + both[n:].T
    inverse_factor(z_ref, rest, lower, aug, factor_work)

    height = modes_ref.shape[0]
    own_rows = span(core * height, height, 16)
    total = jnp.zeros(modes_ref.shape, F32)
    for block in range(blocks):
        here = slice(block * width, (block + 1) * width)
        value_high, value_low = split(lifted[:, here])
        q_low = jnp.concatenate(
            [times_factor(value_high, value_low, rows) for rows in halves], axis=0
        ).astype(BF16)
        total = total + dot_low(a_ref[own_rows, here], q_low, NT)
    modes_ref[...] = total.astype(BF16)
    reduction.finish()


def on_device(bases, start):
    count = lax.axis_size("batch")
    width, n = start.shape
    all_columns = width * count
    height = bases.shape[0] // count
    flat = all_columns * n // 2 // 128
    sems = lambda number: [pltpu.SemaphoreType.DMA((number,))] * 2
    slots = []
    for unit in UNITS:
        slots.append(pltpu.VMEM((3, 16 * unit, 128), BF16))
        slots.append(pltpu.VMEM((len(PLANE), unit, 128), F32))
    return pl.pallas_call(
        whole_kernel,
        out_shape=jax.ShapeDtypeStruct((height, n), BF16),
        in_specs=[pl.BlockSpec(memory_space=pl.ANY), VMEM_SPEC],
        out_specs=VMEM_SPEC,
        scratch_shapes=[
            pltpu.VMEM(bases.shape, BF16),
            pltpu.VMEM((n, width), F32),
            pltpu.VMEM((2 * height, all_columns), BF16),
            pltpu.VMEM((flat // 256, 256, 128), F32),
            pltpu.VMEM((5, 8, 128), F32),
            pltpu.VMEM((4, 3, 8, 128), F32),
            pltpu.VMEM((2, flat, 128), F32),
            pltpu.VMEM((2, flat, 128), BF16),
            pltpu.VMEM((2, flat, 128), F32),
            pltpu.VMEM((2, flat, 128), F32),
            pltpu.VMEM((2, flat, 128), F32),
            pltpu.VMEM((n, all_columns), F32),
            pltpu.VMEM((n, n), F32),
            pltpu.VMEM((n, n), F32),
            pltpu.VMEM((n, n), F32),
            pltpu.VMEM((NB, 2 * NB), F32),
            pltpu.VMEM((NB, 2 * NB), F32),
            *slots, *slots,
            *sems(EXCHANGE_COPIES), *sems(REDUCE_COPIES), *sems(REDUCE_COPIES),
            *sems(ENERGY_COPIES),
            pltpu.SemaphoreType.DMA((4,)),
            pltpu.SemaphoreType.REGULAR,
        ],
        compiler_params=pltpu.CompilerParams(
            collective_id=0, has_side_effects=True, vmem_limit_bytes=66_000_000
        ),
    )(bases, start)


def solution(mesh):
    in_specs = (P("rows", "batch"), P("batch", None))
    out_specs = P(("rows", "batch"), None)
    return jax.shard_map(
        on_device, mesh=mesh, in_specs=in_specs, out_specs=out_specs, check_vma=False
    )
```

```python
import functools

import jax
import jax.numpy as jnp
from jax import lax
from jax.experimental import pallas as pl
from jax.experimental.pallas import tpu as pltpu
from jax.sharding import PartitionSpec as P

NB = 128
GROUPS = 8
RING = 4
CHIPS = 64
ORDERS = (("x", "y", "z"), ("y", "z", "x"), ("z", "x", "y")) * 2
UNITS = (16, 8, 8, 8, 16, 8)
COLOURS = len(UNITS)
PARTNER_ORDER = (1, 7, 3, 5, 2, 6, 4)
HIGHEST = lax.Precision.HIGHEST
VMEM_SPEC = pl.BlockSpec(memory_space=pltpu.VMEM)
F32, BF16 = jnp.float32, jnp.bfloat16
NN, NT, TN = ((1,), (0,)), ((1,), (1,)), ((0,), (0,))


def dot_f32(left, right, dims):
    return lax.dot_general(
        left, right, (dims, ((), ())), precision=HIGHEST, preferred_element_type=F32
    )


def dot_low(left, right, dims):
    return lax.dot_general(left, right, (dims, ((), ())), preferred_element_type=F32)


def split(value):
    high = value.astype(BF16)
    return high, (value - high.astype(F32)).astype(BF16)


def stack(value):
    return jnp.concatenate(split(value), axis=0)


def fold(value):
    half = value.shape[0] // 2
    return value[:half] + value[half:]


def span(start, size, unit):
    return pl.ds(pl.multiple_of(start, unit), size)


def position():
    rows, batch = lax.axis_index("rows"), lax.axis_index("batch")
    return {
        "x": rows // 2 % 4,
        "y": batch % 4,
        "z": batch // 4 * 2 + rows // 8,
        "core": rows % 2,
    }


def device_at(pos):
    return {
        "rows": pos["z"] % 2 * 8 + pos["x"] * 2 + pos["core"],
        "batch": pos["z"] // 2 * 4 + pos["y"],
    }


def ring_peer(pos, axis, distance):
    there = dict(pos)
    there[axis] = (pos[axis] + distance) % RING
    return there


def shifted(pos, shifts):
    there = dict(pos)
    for axis, distance in shifts.items():
        if distance:
            there[axis] = (pos[axis] + distance) % RING
    return there


def axis_peers(pos):
    return [ring_peer(pos, axis, d) for axis in "xyz" for d in (1, 2, 3)]


def sibling(pos):
    there = dict(pos)
    there["core"] = 1 - pos["core"]
    return there


def greet(peers, work):
    barrier = pltpu.get_barrier_semaphore()
    for peer in peers:
        pl.semaphore_signal(
            barrier, inc=1, device_id=device_at(peer), device_id_type=pl.DeviceIdType.MESH
        )
    work()
    pl.semaphore_wait(barrier, len(peers))


class Copies:
    def __init__(self, send_sem, recv_sem):
        self.send_sem, self.recv_sem = send_sem, recv_sem

    def copy(self, index, src, dst, peer):
        return pltpu.make_async_remote_copy(
            src_ref=src, dst_ref=dst,
            send_sem=self.send_sem.at[index], recv_sem=self.recv_sem.at[index],
            device_id=device_at(peer), device_id_type=pl.DeviceIdType.MESH,
        )


def batch_partners(pos, batch, count):
    partners = []
    for distance in range(1, count):
        other = (batch + distance) % count
        there = dict(pos)
        there["y"] = other % 4
        there["z"] = other // 4 * 2 + pos["z"] % 2
        partners.append(there)
    return partners


def exchange(pos, bases_ref, turned, a_ref, q_ref, energy, copies, own_sem):
    core, x = pos["core"], pos["x"]
    batch = lax.axis_index("batch")
    count = lax.axis_size("batch")
    height = bases_ref.shape[0] // count
    width = bases_ref.shape[1]
    quarter = 64
    partners = batch_partners(pos, batch, count)
    x_peers = [ring_peer(pos, "x", d) for d in (1, 2, 3)]
    made = []

    def start(src, dst, peer):
        copy = copies.copy(len(made), src, dst, peer)
        copy.start()
        made.append(copy)
        return copy

    own_rows = span(core * height, height, 16)
    mine = span(x * quarter, quarter, 8)
    turned_rows = span(core * 256 + x * quarter, quarter, 8)

    def columns(which):
        return span(which * width, width, 128)

    def block_rows(which):
        return span(which * height, height, 16)

    def piece(which, half):
        return q_ref.at[which * 2 + half, mine, :]

    own_start = []
    for half in range(2):
        own = pltpu.make_async_copy(
            turned.at[turned_rows, half * 128:(half + 1) * 128], piece(batch, half),
            own_sem.at[half],
        )
        own.start()
        own_start.append(own)
    start_in = [
        [start(turned.at[turned_rows, half * 128:(half + 1) * 128], piece(batch, half), there)
         for half in range(2)]
        for there in (partners[d - 1] for d in PARTNER_ORDER)
    ]
    x_in = [
        start(turned.at[turned_rows, half * 128:(half + 1) * 128], piece(batch, half), there)
        for half in range(2) for there in x_peers
    ]
    block_in = [
        start(bases_ref.at[block_rows((batch + d) % count), :],
              a_ref.at[own_rows, columns(batch)], partners[d - 1])
        for d in PARTNER_ORDER
    ]
    own_block = pltpu.make_async_copy(
        bases_ref.at[block_rows(batch), :], a_ref.at[own_rows, columns(batch)], own_sem.at[2]
    )
    own_block.start()
    aside = [
        start(bases_ref.at[block_rows(batch), :], a_ref.at[own_rows, columns(batch)],
              sibling(pos))
    ]

    def add_square(step, total):
        value = bases_ref[span(step * 64, 64, 64), :].astype(F32)
        value = value * value
        return total + jnp.sum(value.reshape(8, 8, 2 * 128), axis=0)

    total = lax.fori_loop(
        0, bases_ref.shape[0] // 64, add_square, jnp.zeros((8, 2 * 128), F32)
    )
    total = total[:, :128] + total[:, 128:]

    energy.begin(total)
    for distance, pair in zip(PARTNER_ORDER, start_in):
        for copy in pair:
            copy.wait_recv()
        other = (batch + count - distance) % count
        block = q_ref.at[span(other * 2, 2, 2), mine, :]
        x_in += [start(block, block, there) for there in x_peers]
    for copy in own_start:
        copy.wait()
    own_block.wait()
    for distance, copy in zip(PARTNER_ORDER, block_in):
        copy.wait_recv()
        other = (batch + count - distance) % count
        block = a_ref.at[own_rows, columns(other)]
        aside.append(start(block, block, sibling(pos)))
    for copy in x_in + aside:
        copy.wait_recv()
    for copy in made:
        copy.wait_send()


EXCHANGE_COPIES = 14 + 6 + 7 + 1 + 21 + 7


class Energy:
    def __init__(self, pos, sums, slots, copies):
        self.sums, self.slots, self.copies = sums, slots, copies
        self.rings = [[ring_peer(pos, axis, d) for d in (1, 2, 3)] for axis in "xyz"]
        self.rings.append([sibling(pos)])

    def copy(self, stage, slot):
        return self.copies.copy(
            3 * stage + slot, self.sums.at[stage], self.slots.at[stage, slot],
            self.rings[stage][slot],
        )

    def begin(self, total):
        self.sums[0] = total
        for slot in range(3):
            self.copy(0, slot).start()

    def step(self, stage):
        total = self.sums[stage]
        for slot in range(len(self.rings[stage])):
            self.copy(stage, slot).wait()
            total = total + self.slots[stage, slot]
        self.sums[stage + 1] = total
        if stage < 3:
            for slot in range(len(self.rings[stage + 1])):
                self.copy(stage + 1, slot).start()

    def value(self):
        return jnp.sum(self.sums[4], keepdims=True)


ENERGY_COPIES = 10


PLANE = [(a, b) for a in range(RING) for b in range(RING) if a or b]


class Reduction:
    def __init__(self, pos, part, part_low, work, out, slots, copies, forward):
        self.pos, self.part, self.work, self.out = pos, part, work, out
        self.part_low, self.forward = part_low, forward
        self.slots, self.copies = slots, copies
        self.base = [CHIPS * sum(UNITS[:k]) for k in range(COLOURS)]

    def first(self, k):
        return self.pos[ORDERS[k][0]]

    def origin(self, k):
        return self.base[k] + self.first(k) * 16 * UNITS[k]

    def place(self, k, a, b):
        _, one, two = ORDERS[k]
        index = (self.pos[one] + a) % RING * RING + (self.pos[two] + b) % RING
        return self.origin(k) + index * UNITS[k]

    def peer(self, k, a, b):
        return shifted(self.pos, {ORDERS[k][1]: a, ORDERS[k][2]: b})

    def ring_peer(self, k, d):
        return ring_peer(self.pos, ORDERS[k][0], d)

    def block(self, start, size):
        return self.out.at[self.pos["core"], span(start, size, 8), :]

    def ring_sum(self, k, d):
        size = 16 * UNITS[k]
        target = (self.first(k) + d) % RING
        return self.copies.copy(
            40 * k + d - 1, self.part_low.at[span(self.base[k] + target * size, size, 16), :],
            self.slots[2 * k].at[d - 1], self.ring_peer(k, d),
        )

    def plane_sum(self, k, slot):
        a, b = PLANE[slot]
        return self.copies.copy(
            40 * k + 3 + slot, self.work.at[span(self.place(k, a, b), UNITS[k], 8), :],
            self.slots[2 * k + 1].at[slot], self.peer(k, a, b),
        )

    def plane_gather(self, k, slot):
        block = self.block(self.place(k, 0, 0), UNITS[k])
        return self.copies.copy(40 * k + 18 + slot, block, block, self.peer(k, *PLANE[slot]))

    def ring_gather(self, k, d):
        block = self.block(self.origin(k), 16 * UNITS[k])
        return self.copies.copy(40 * k + 33 + d - 1, block, block, self.ring_peer(k, d))

    def aside_copy(self, k, d):
        size = 16 * UNITS[k]
        sender = (self.first(k) + RING - d) % RING
        block = self.block(self.base[k] + sender * size, size)
        return self.copies.copy(40 * k + 36 + d, block, block, sibling(self.pos))

    def start(self, k):
        for d in (1, 2, 3):
            self.ring_sum(k, d).start()

    def step(self, number, colours=range(COLOURS)):
        for k in colours:
            if number == 0:
                for d in (1, 2, 3):
                    self.ring_sum(k, d).wait_recv()
                here = span(self.origin(k), 16 * UNITS[k], 8)
                value = self.part[here, :]
                for d in range(3):
                    value = value + self.slots[2 * k][d].astype(F32)
                self.work[here, :] = value
                for slot in range(len(PLANE)):
                    self.plane_sum(k, slot).start()
            elif number == 1:
                here = span(self.place(k, 0, 0), UNITS[k], 8)
                value = self.work[here, :]
                for slot in range(len(PLANE)):
                    self.plane_sum(k, slot).wait_recv()
                    value = value + self.slots[2 * k + 1][slot]
                self.out[self.pos["core"], here, :] = value
                for slot in range(len(PLANE)):
                    self.plane_gather(k, slot).start()
            elif number == 2:
                for slot in range(len(PLANE)):
                    self.plane_gather(k, slot).wait_recv()
                for d in (1, 2, 3):
                    self.ring_gather(k, d).start()
                if self.forward:
                    self.aside_copy(k, 0).start()
            else:
                for d in (1, 2, 3):
                    self.ring_gather(k, d).wait_recv()
                    if self.forward:
                        self.aside_copy(k, d).start()

    def join(self):
        for k in range(COLOURS):
            for d in range(4):
                self.aside_copy(k, d).wait_recv()

    def finish(self):
        for k in range(COLOURS):
            if self.forward:
                for d in range(4):
                    self.aside_copy(k, d).wait_send()
            for d in (1, 2, 3):
                self.ring_sum(k, d).wait_send()
                self.ring_gather(k, d).wait_send()
            for slot in range(len(PLANE)):
                self.plane_sum(k, slot).wait_send()
                self.plane_gather(k, slot).wait_send()


REDUCE_COPIES = 40 * COLOURS


def apply_gram(a_ref, q_block, combine, reduction):
    chunks = a_ref.shape[1] // 128
    q = jnp.concatenate([q_block(chunk) for chunk in range(chunks)], axis=1)
    inner = stack(fold(dot_low(stack(q), a_ref[...], NT)))
    ready = 0
    for block in range(chunks // 2):
        value = fold(dot_low(inner, a_ref[:, block * 256:(block + 1) * 256], NN))
        for half in range(2):
            chunk = 2 * block + half
            share = combine(value[:, half * 128:(half + 1) * 128], chunk)
            here = slice(chunk * 256, (chunk + 1) * 256)
            reduction.part[here, :] = share
            reduction.part_low[here, :] = share.astype(BF16)
        while ready < COLOURS and CHIPS * sum(UNITS[:ready + 1]) <= (block + 1) * 512:
            reduction.start(ready)
            ready += 1


def factor_block(aug, work, between=lambda: None):
    row = lax.broadcasted_iota(jnp.int32, (8, NB), 0)
    height = 8 * GROUPS
    for panel in range(NB // height):
        low = height * panel
        left = [aug[low + 8 * g:low + 8 * g + 8, :NB] for g in range(GROUPS)]
        right = [aug[low + 8 * g:low + 8 * g + 8, NB:] for g in range(GROUPS)]
        for s in range(GROUPS):
            rest = range(s, GROUPS)
            lane = low + 8 * s
            cols = {
                (g, k): jnp.broadcast_to(left[g][:, lane + k:lane + k + 1], (8, NB))
                for g in rest for k in range(8)
            }
            pivots = jnp.zeros((8, NB), F32)
            for k in range(8):
                pivot = jnp.broadcast_to(cols[s, k][k:k + 1, :], (8, NB))
                inverse = 1.0 / pivot
                pivots = jnp.where(row == k, pivot, pivots)
                mult = {g: cols[g, k] * inverse for g in rest}
                mult[s] = jnp.where(row > k, mult[s], 0.0)
                for j in range(k + 1, 8):
                    value = jnp.broadcast_to(cols[s, j][k:k + 1, :], (8, NB))
                    for g in rest:
                        cols[g, j] = cols[g, j] - mult[g] * value
                left_row = jnp.broadcast_to(left[s][k:k + 1, :], (8, NB))
                right_row = jnp.broadcast_to(right[s][k:k + 1, :], (8, NB))
                for g in rest:
                    left[g] = left[g] - mult[g] * left_row
                    right[g] = right[g] - mult[g] * right_row
            scale = lax.rsqrt(pivots)
            work[lane:lane + 8, :NB] = left[s] * scale
            work[lane:lane + 8, NB:] = right[s] * scale
        if low + height < NB:
            rows = work[low:low + height, :]
            aug[low + height:, :] = (
                aug[low + height:, :] - dot_f32(rows[:, :NB], rows, TN)[low + height:, :])
            between()


def inverse_factor(z_ref, rest, lower, aug, work, hooks={}):
    n = rest.shape[0]
    blocks = n // NB
    z_ref[...] = jnp.zeros_like(z_ref)
    row = lax.broadcasted_iota(jnp.int32, (NB, NB), 0)
    col = lax.broadcasted_iota(jnp.int32, (NB, NB), 1)

    @pl.loop(0, blocks)
    def _(j):
        here = span(j * NB, NB, NB)
        aug[:, :NB] = rest[here, here]
        aug[:, NB:] = jnp.where(row == col, 1.0, 0.0)

        def between():
            for block in range(blocks):
                if (block, 0) in hooks:
                    pl.when(j == block)(hooks[block, 0])

        factor_block(aug, work, between)
        for block in range(blocks):
            @pl.when(j == block)
            def _():
                low, high = block * NB, (block + 1) * NB
                inverse = jnp.where(row >= col, work[:, NB:], 0.0)
                z_ref[low:high, low:high] = inverse
                if high < n:
                    column = dot_f32(rest[high:, low:high], inverse, NT)
                    lower[high:, low:high] = column
                    rest[high:, high:] = rest[high:, high:] - dot_f32(column, column, NT)
                if low:
                    z_ref[low:high, :low] = -dot_f32(
                        inverse, dot_f32(lower[low:high, :low], z_ref[:low, :low], NN), NN)
                hooks.get((block, 1), lambda: None)()


def whole_kernel(bases_ref, start_ref, modes_ref, *scratch):
    (slab, turned, a_ref, q_ref, e_sums, e_slots, part, part_low, work, first, second, lifted,
     z_ref, rest, lower, aug, factor_work) = scratch[:17]
    slots, sems, own_sem, entered = scratch[17:-10], scratch[-10:-2], scratch[-2], scratch[-1]
    pos = position()
    core = pos["core"]
    load = pltpu.make_async_copy(bases_ref, slab, own_sem.at[3])
    load.start()
    def turn():
        turned[...] = start_ref[...].T

    peers = batch_partners(pos, lax.axis_index("batch"), lax.axis_size("batch"))
    peers += [ring_peer(pos, "x", d) for d in (1, 2, 3)]
    peers += [ring_peer(pos, "z", d) for d in (1, 3)] + [sibling(pos)]
    greet(peers, turn)
    for peer in axis_peers(pos):
        pl.semaphore_signal(
            entered, inc=1, device_id=device_at(peer), device_id_type=pl.DeviceIdType.MESH
        )
    load.wait()
    energy = Energy(pos, e_sums, e_slots, Copies(*sems[6:]))
    exchange(pos, slab, turned, a_ref, q_ref, energy, Copies(*sems[:2]), own_sem)
    n, all_columns = lifted.shape
    chunks = all_columns // NB

    reduction = Reduction(
        pos, part.at[0], part_low.at[0], work.at[0], first, slots[:2 * COLOURS],
        Copies(*sems[2:4]), False,
    )
    early = reduction
    apply_gram(a_ref, lambda chunk: q_ref[chunk], lambda value, chunk: value, reduction)
    pl.semaphore_wait(entered, 9)
    for number in range(4):
        energy.step(number)
        reduction.step(number)
    early.finish()
    scale = all_columns / energy.value()
    for chunk in range(chunks):
        here = slice(chunk * 256, (chunk + 1) * 256)
        first[core, here, :] = first[core, here, :] * scale + q_ref[chunk]
    over = Copies(*sems[2:4]).copy(
        36, first.at[core], first.at[core], sibling(pos)
    )
    over.start()

    reduction = Reduction(
        pos, part.at[1], part_low.at[1], work.at[1], second, slots[2 * COLOURS:],
        Copies(*sems[4:6]), True,
    )

    def first_block(chunk):
        return first[core, chunk * 256:(chunk + 1) * 256, :]

    apply_gram(
        a_ref, first_block,
        lambda value, chunk: value * scale + first_block(chunk) * (1.0 / CHIPS), reduction,
    )

    def side(ref, half):
        return jnp.concatenate(
            [ref[half, chunk * 256:(chunk + 1) * 256, :] for chunk in range(chunks)], axis=1)

    over.wait()
    low = jnp.concatenate([side(first, half).astype(BF16) for half in range(2)], axis=0)
    rest[...] = dot_low(low, low, NT)
    places = [(0, 0), (0, 1), (1, 0), (1, 1), (2, 0), (2, 1)]
    parts = [(number, range(3 * part, 3 * part + 3)) for number in range(3) for part in range(2)]
    inverse_factor(
        z_ref, rest, lower, aug, factor_work,
        {place: functools.partial(reduction.step, *part) for place, part in zip(places, parts)},
    )
    reduction.step(3)
    reduction.join()

    def times_factor(value_high, value_low, rows):
        z_stack = stack(z_ref[rows, :rows.stop])
        z_high = z_stack[:rows.stop - rows.start]
        return (fold(dot_low(z_stack, value_high[:rows.stop], NN))
                + dot_low(z_high, value_low[:rows.stop], NN))

    halves = [slice(0, n // 2), slice(n // 2, n)]
    blocks = 4
    width = all_columns // blocks
    rest[...] = jnp.zeros_like(rest)
    for block in range(blocks):
        value = jnp.concatenate(
            [jnp.concatenate(
                [second[half, chunk * 256:(chunk + 1) * 256, :]
                 for chunk in range(block * chunks // blocks, (block + 1) * chunks // blocks)],
                axis=1) for half in range(2)], axis=0)
        value_high, value_low = split(value)
        value = jnp.concatenate(
            [times_factor(value_high, value_low, rows) for rows in halves], axis=0)
        lifted[:, block * width:(block + 1) * width] = value
    both = stack(lifted[...])
    both = dot_low(both, both[:n], NT)
    rest[...] = both[:n] + both[n:] + both[n:].T
    inverse_factor(z_ref, rest, lower, aug, factor_work)

    height = modes_ref.shape[0]
    own_rows = span(core * height, height, 16)
    total = jnp.zeros(modes_ref.shape, F32)
    for block in range(blocks):
        here = slice(block * width, (block + 1) * width)
        value_high, value_low = split(lifted[:, here])
        q_low = jnp.concatenate(
            [times_factor(value_high, value_low, rows) for rows in halves], axis=0
        ).astype(BF16)
        total = total + dot_low(a_ref[own_rows, here], q_low, NT)
    modes_ref[...] = total.astype(BF16)
    reduction.finish()


def on_device(bases, start):
    count = lax.axis_size("batch")
    width, n = start.shape
    all_columns = width * count
    height = bases.shape[0] // count
    flat = all_columns * n // 2 // 128
    sems = lambda number: [pltpu.SemaphoreType.DMA((number,))] * 2
    slots = []
    for unit in UNITS:
        slots.append(pltpu.VMEM((3, 16 * unit, 128), BF16))
        slots.append(pltpu.VMEM((len(PLANE), unit, 128), F32))
    return pl.pallas_call(
        whole_kernel,
        out_shape=jax.ShapeDtypeStruct((height, n), BF16),
        in_specs=[pl.BlockSpec(memory_space=pl.ANY), VMEM_SPEC],
        out_specs=VMEM_SPEC,
        scratch_shapes=[
            pltpu.VMEM(bases.shape, BF16),
            pltpu.VMEM((n, width), F32),
            pltpu.VMEM((2 * height, all_columns), BF16),
            pltpu.VMEM((flat // 256, 256, 128), F32),
            pltpu.VMEM((5, 8, 128), F32),
            pltpu.VMEM((4, 3, 8, 128), F32),
            pltpu.VMEM((2, flat, 128), F32),
            pltpu.VMEM((2, flat, 128), BF16),
            pltpu.VMEM((2, flat, 128), F32),
            pltpu.VMEM((2, flat, 128), F32),
            pltpu.VMEM((2, flat, 128), F32),
            pltpu.VMEM((n, all_columns), F32),
            pltpu.VMEM((n, n), F32),
            pltpu.VMEM((n, n), F32),
            pltpu.VMEM((n, n), F32),
            pltpu.VMEM((NB, 2 * NB), F32),
            pltpu.VMEM((NB, 2 * NB), F32),
            *slots, *slots,
            *sems(EXCHANGE_COPIES), *sems(REDUCE_COPIES), *sems(REDUCE_COPIES),
            *sems(ENERGY_COPIES),
            pltpu.SemaphoreType.DMA((4,)),
            pltpu.SemaphoreType.REGULAR,
        ],
        compiler_params=pltpu.CompilerParams(
            collective_id=0, has_side_effects=True, vmem_limit_bytes=66_000_000
        ),
    )(bases, start)


def solution(mesh):
    in_specs = (P("rows", "batch"), P("batch", None))
    out_specs = P(("rows", "batch"), None)
    return jax.shard_map(
        on_device, mesh=mesh, in_specs=in_specs, out_specs=out_specs, check_vma=False
    )
```
